128 devices in a mesh: qn: 4 (over y), blk: 32 (over z, x, core).
Axes of the slice: x: 4, y: 4, z: 4, core: 2. Of those that a mesh axis runs over, the one named last changes fastest.
Arguments:
- wavefunction: bfloat16 [4096, 256, 256], P(('qn', 'blk')), may hold values from -6 to 6
- pair_left: int32 [4096], P(('qn', 'blk')), may hold values from 0 to 1
- pair_right: int32 [4096], P(('qn', 'blk')), may hold values from 0 to 1
- left_env: bfloat16 [256, 8, 256, 256], P(('qn', 'blk')), may hold values from -0.375 to 0.375
- left_dims: int32 [256], P(('qn', 'blk')), may hold values from 128 to 256, as said below
- right_env: bfloat16 [256, 8, 256, 256], P(('qn', 'blk')), may hold values from -0.125 to 0.125
- right_dims: int32 [256], P(('qn', 'blk')), may hold values from 128 to 256, as said below
Outputs:
- applied: bfloat16 [4096, 256, 256], P(('qn', 'blk'))
The draws below stay inside these ranges and needn't reach their ends.
Inputs may be any that keep to these rules, and one draw needn't show every extreme that they name: `left_dims`: multiples of 8; the largest entry equals 256. `right_dims`: multiples of 8; the largest entry equals 256.
All inputs are finite; a program needn't handle non-finite values.
Results may differ from the reference program's by a relative error of at most 0.005.
Values may be sent and summed in bfloat16 or wider, within the bound.
No kernel may reach another device: no remote copies, remote signals or barrier semaphores. Data moves between devices by JAX's collectives and lax.ppermute only.
A program may use at most 384 MiB of HBM per device.

```python
import jax
import jax.numpy as jnp
from jax import lax

BW = 256
NT = 8
SEC_DEV = 2
SLOTS = 32
SECTORS = 256
BLOCKS = 4096
N_QN = 4
N_BLK = 32


def sector_sizes(key):
    first_key, second_key = jax.random.split(key)
    levels = jax.random.randint(first_key, (SECTORS,), BW // 16, BW // 8 + 1) * 8
    chosen_spot = jax.random.randint(second_key, (), 0, SECTORS)
    return jnp.where(jnp.arange(SECTORS) == chosen_spot, BW, levels).astype(jnp.int32)


def draw_left_dims(key, part):
    return sector_sizes(jax.random.fold_in(key, 11))


def draw_right_dims(key, part):
    return sector_sizes(jax.random.fold_in(key, 23))


def plant(entries, rng, low, high):
    shape = entries.shape
    place = [jax.random.randint(jax.random.fold_in(rng, axis), (), 0, shape[axis]) for axis in range(len(shape))]
    entries = entries.at[tuple(place)].set(low)
    longest = shape.index(max(shape))
    place[longest] = (place[longest] + 1) % shape[longest]
    return entries.at[tuple(place)].set(high)


def block_scale(key, extent, shards, smallest, high):
    level, own = 1.0, jax.random.fold_in(key, 6)
    for position, shards_of in shards:
        heights = jnp.exp(jax.random.uniform(jax.random.fold_in(own, position), (shards_of,), jnp.float32, smallest / len(shards), high / len(shards)))
        level = level * jnp.repeat(heights, extent[position] // shards_of).reshape([-1 if axis == position else 1 for axis in range(len(extent))])
    return level


def scatter_about(rng, extent, deviation, limit, pieces=(), held_as=jnp.bfloat16):
    level = block_scale(rng, extent, pieces, -0.22, 0.18) if pieces else 1.0
    drawn = jax.random.normal(rng, extent, jnp.float32) * deviation * level
    return jnp.minimum(jnp.maximum(drawn, -limit), limit).astype(held_as)


def setup_inputs(seed: int = 0) -> dict:
    seeds = jax.random.split(jax.random.key(seed), 8)
    wavefunction = scatter_about(seeds[0], (BLOCKS, BW, BW), 1.0, 6.0, ((0, 128),))
    pair_left = plant(jax.random.randint(seeds[1], (BLOCKS,), 0, SEC_DEV), jax.random.fold_in(seeds[1], 1), 0, SEC_DEV - 1).astype(jnp.int32)
    pair_right = plant(jax.random.randint(seeds[2], (BLOCKS,), 0, SEC_DEV), jax.random.fold_in(seeds[2], 1), 0, SEC_DEV - 1).astype(jnp.int32)
    left_env = scatter_about(seeds[3], (SECTORS, NT, BW, BW), BW ** -0.5, 0.375, ((0, 128),))
    left_dims = draw_left_dims(jax.random.fold_in(seeds[7], 71), 0)
    right_env = scatter_about(seeds[5], (SECTORS, NT, BW, BW), (NT * BW) ** -0.5, 0.125, ((0, 128),))
    right_dims = draw_right_dims(jax.random.fold_in(seeds[7], 71), 0)
    return dict(wavefunction=wavefunction, pair_left=pair_left, pair_right=pair_right, left_env=left_env, left_dims=left_dims, right_env=right_env, right_dims=right_dims)


def reference(wavefunction, pair_left, pair_right, left_env, left_dims, right_env, right_dims):
    device_count = N_QN * N_BLK
    per_group = SLOTS // N_QN
    per_peer = SLOTS // N_BLK
    slot_index = jnp.arange(SLOTS, dtype=jnp.int32)
    row_index = jnp.arange(BW, dtype=jnp.int32)

    def one_sender(sender):
        group_here = sender // N_BLK
        block_here = sender % N_BLK
        target_group = slot_index // per_group
        left_owner = target_group * N_BLK + block_here
        received = group_here * per_group + slot_index % per_group
        right_owner = target_group * N_BLK + received // per_peer
        offset = sender * SLOTS
        blocks = lax.dynamic_slice_in_dim(wavefunction, offset, SLOTS, 0)
        left_pick = lax.dynamic_slice_in_dim(pair_left, offset, SLOTS, 0)
        right_pick = lax.dynamic_slice_in_dim(pair_right, offset, SLOTS, 0)
        left_sector = (left_owner * SEC_DEV + left_pick).astype(jnp.int32)
        right_sector = (right_owner * SEC_DEV + right_pick).astype(jnp.int32)
        rows_live = left_dims[left_sector]
        cols_live = right_dims[right_sector]
        keep = (row_index[None, :, None] < rows_live[:, None, None]) & (row_index[None, None, :] < cols_live[:, None, None])
        masked = jnp.where(keep, blocks, jnp.zeros_like(blocks))
        running = jnp.zeros((SLOTS, BW, BW), jnp.float32)
        for term_index in range(NT):
            left_block = left_env[left_sector, term_index].astype(jnp.float32)
            partial_value = jnp.einsum("sij,sjk->sik", left_block, masked.astype(jnp.float32)).astype(jnp.bfloat16)
            right_block = right_env[right_sector, term_index].astype(jnp.float32)
            running = running + jnp.einsum("sij,sjk->sik", partial_value.astype(jnp.float32), right_block)
        home = (right_owner * SLOTS + block_here * per_peer + received % per_peer).astype(jnp.int32)
        return running.astype(jnp.bfloat16), home

    results, homes = lax.map(one_sender, jnp.arange(device_count, dtype=jnp.int32))
    applied = jnp.zeros((device_count * SLOTS, BW, BW), jnp.bfloat16)
    return applied.at[homes.reshape(-1)].set(results.reshape(-1, BW, BW))
```

```python
import jax
import jax.numpy as jnp
import numpy as np
from jax import lax
from jax.experimental import pallas as pl
from jax.experimental.pallas import tpu as pltpu
from jax.sharding import Mesh, PartitionSpec as P

AXES = ("y", "z", "x", "c")
OFFSETS = (0, 3, 1, 2)
BF16 = jnp.bfloat16


def ring_positions():
    rows = []
    for y, z, x, c in np.ndindex(4, 4, 4, 2):
        rows.append([(z + o) % 4 for o in OFFSETS] + [(x + o) % 4 for o in OFFSETS] + [y, z, x, c])
    return np.asarray(rows, np.int32)


def exchange(array, axis):
    return lax.all_to_all(array, axis, split_axis=0, concat_axis=0, tiled=True)


def shift(array, axis, step, size=4):
    return lax.ppermute(array, axis, [(i, (i + step) % size) for i in range(size)])


def both_ways(array, axis):
    return shift(array, axis, 1), shift(array, axis, 3)


def onward(from_low, from_high, axis):
    half = from_low.shape[1] // 2
    return shift(from_low[:, :half], axis, 1), shift(from_high[:, half:], axis, 3)


def combine(where, meta, psi, lefts, rights, first):
    width = psi.shape[-1]
    depth = sum(a.shape[1] for a in lefts[0])
    terms = depth // width
    count = len(lefts)
    left_parts = [a for group in lefts for a in group]
    right_parts = [a for group in rights for a in group]

    def place(i, where):
        source, k = i // count, i % count
        g = where[source // 2]
        c_r = where[11] ^ (source % 2)
        x_j = where[4 + first + k]
        return g, c_r, x_j, k

    def picks(i, where, meta):
        g, c_r, x_j, k = place(i, where)
        y, z, x, c = where[8], where[9], where[10], where[11]
        sender = ((g * 4 + z) * 4 + x_j) * 2 + c
        slot = y * 8 + x * 2 + c_r
        left = meta[sender * 128 + slot]
        right = meta[sender * 128 + 32 + slot]
        rows = meta[(((y * 4 + z) * 4 + x_j) * 2 + c) * 128 + 64 + left]
        cols = meta[(((y * 4 + g) * 4 + x) * 2 + c_r) * 128 + 66 + right]
        return left, right, rows, cols

    def psi_index(i, where, meta):
        g, c_r, x_j, k = place(i, where)
        return (g * 4 + x_j) * 2 + c_r, 0, 0

    def out_index(i, where, meta):
        g, c_r, x_j, k = place(i, where)
        return (g * 2 + c_r) * count + k, 0, 0

    def kernel(where, meta, psi_ref, *refs):
        left_refs = refs[: len(left_parts)]
        right_refs = refs[len(left_parts) : len(left_parts) + len(right_parts)]
        out_ref, right_buf, partial, sems = refs[len(left_parts) + len(right_parts) :]
        i = pl.program_id(0)
        steps = pl.num_programs(0)

        def fetch(step, go):
            _, right, _, _ = picks(step, where, meta)
            slot = lax.rem(step, 2)
            at = 0
            for source, group in enumerate(rights):

                @pl.when(step // count == source)
                def _(at=at, group=group):
                    row = 0
                    for n in range(len(group)):
                        size = group[n].shape[1]
                        copy = pltpu.make_async_copy(
                            right_refs[at + n].at[right],
                            right_buf.at[slot, pl.ds(row, size)],
                            sems.at[slot, n],
                        )
                        copy.start() if go else copy.wait()
                        row += size

                at += len(group)

        @pl.when(i == 0)
        def _():
            fetch(i, True)

        @pl.when(i + 1 < steps)
        def _():
            fetch(i + 1, True)

        left, _, rows, cols = picks(i, where, meta)
        keep = (lax.broadcasted_iota(jnp.int32, (width, width), 0) < rows) & (
            lax.broadcasted_iota(jnp.int32, (width, width), 1) < cols
        )
        masked = jnp.where(keep, psi_ref[0].astype(jnp.float32), 0.0).astype(BF16)

        def first_half(group):
            t = 0
            for ref in group:
                for n in range(ref.shape[1] // width):
                    block = ref[left, pl.ds(n * width, width)]
                    product = jnp.dot(block, masked, preferred_element_type=jnp.float32)
                    partial[:, t * width : (t + 1) * width] = product.astype(BF16)
                    t += 1

        at = 0
        for k, group in enumerate(lefts):
            here = left_refs[at : at + len(group)]
            at += len(group)
            if count == 1:
                first_half(here)
            else:
                pl.when(i % count == k)(lambda here=here: first_half(here))

        fetch(i, False)
        total = jnp.dot(partial[...], right_buf[lax.rem(i, 2)], preferred_element_type=jnp.float32)
        out_ref[0] = total.astype(BF16)

    blocks = 2 * 4 * count
    whole = lambda i, where, meta: (0, 0, 0)
    parts = max(len(group) for group in rights)
    moved = blocks * (depth * width * 2 + 2 * width * width * 2) + count * 2 * depth * width * 2
    return pl.pallas_call(
        kernel,
        out_shape=jax.ShapeDtypeStruct((blocks, width, width), BF16),
        grid_spec=pltpu.PrefetchScalarGridSpec(
            num_scalar_prefetch=2,
            grid=(blocks,),
            in_specs=[pl.BlockSpec((1, width, width), psi_index)]
            + [pl.BlockSpec(a.shape, whole) for a in left_parts]
            + [pl.BlockSpec(memory_space=pl.ANY) for _ in right_parts],
            out_specs=pl.BlockSpec((1, width, width), out_index),
            scratch_shapes=[
                pltpu.VMEM((2, depth, width), BF16),
                pltpu.VMEM((width, depth), BF16),
                pltpu.SemaphoreType.DMA((2, parts)),
            ],
        ),
        compiler_params=pltpu.CompilerParams(
            dimension_semantics=("arbitrary",), vmem_limit_bytes=32 * 2**20
        ),
        cost_estimate=pl.CostEstimate(
            flops=blocks * terms * 4 * width**3, bytes_accessed=moved, transcendentals=0
        ),
        name=f"combine_{first}",
    )(where, meta, psi, *left_parts, *right_parts)


def after(array, *others):
    return lax.optimization_barrier((array, *others))[0]


def body(wavefunction, pair_left, pair_right, left_env, left_dims, right_env, right_dims):
    width = wavefunction.shape[-1]
    sectors, terms = left_env.shape[:2]
    me = lax.axis_index(AXES)
    where = lax.dynamic_index_in_dim(jnp.asarray(ring_positions()), me, 0, keepdims=False)
    mine = jnp.concatenate([pair_left, pair_right, left_dims, right_dims])
    mine = jnp.pad(mine, (0, 128 - mine.shape[0]))
    meta = lax.all_gather(mine, AXES, axis=0, tiled=True)

    left_own = left_env.reshape(sectors, terms * width, width)
    right_own = right_env.reshape(sectors, terms * width, width)
    psi = exchange(wavefunction, ("y", "x"))

    right_low, right_high = both_ways(right_own, "z")
    far = onward(right_low, right_high, "z")
    rights = []
    for group in ((right_own,), (right_low,), (right_high,), far):
        rights.append(group)
        rights.append(tuple(shift(a, "c", 1, 2) for a in group))

    left_low, left_high = both_ways(after(left_own, psi), "x")
    left_far = onward(left_low, left_high, "x")

    def home(first, lefts):
        out = combine(where, meta, psi, lefts, rights, first)
        out = exchange(out, ("z", "c"))
        return out.reshape(4, 2, len(lefts), width, width)

    own = home(0, [(left_own,)])
    near = home(1, [(left_low,), (left_high,)])
    opposite = home(3, [left_far])

    applied = jnp.zeros((4, 4, 2, width, width), BF16)
    for position, piece in ((0, own[:, :, 0]), (1, near[:, :, 0]), (2, near[:, :, 1]), (3, opposite[:, :, 0])):
        applied = lax.dynamic_update_slice(
            applied, piece[:, None], (0, where[4 + position], 0, 0, 0)
        )
    return applied.reshape(wavefunction.shape)


def solution(mesh):
    fine = Mesh(mesh.devices.reshape(4, 4, 4, 2), AXES)
    return jax.shard_map(
        body, mesh=fine, in_specs=P(AXES), out_specs=P(AXES), check_vma=False
    )
```

```python
import jax
import jax.numpy as jnp
import numpy as np
from jax import lax
from jax.experimental import pallas as pl
from jax.experimental.pallas import tpu as pltpu
from jax.sharding import Mesh, PartitionSpec as P

AXES = ("y", "z", "x", "c")
OFFSETS = (0, 3, 1, 2)
BF16 = jnp.bfloat16
BRIEF = pl.CostEstimate(flops=1, bytes_accessed=1, transcendentals=0)
LONG = pl.CostEstimate(flops=10**12, bytes_accessed=1, transcendentals=0)
VMEM = 56 * 2**20


def ring_positions():
    rows = []
    for y, z, x, c in np.ndindex(4, 4, 4, 2):
        seen = [OFFSETS.index((z + o - y) % 4) for o in OFFSETS]
        rows.append(
            [(z + o) % 4 for o in OFFSETS]
            + [(x + o) % 4 for o in OFFSETS]
            + [32 * s + y * 8 + x * 2 for s in seen]
            + [c]
        )
    return np.asarray(rows, np.int32)


def exchange(array, axis):
    return lax.all_to_all(array, axis, split_axis=0, concat_axis=0, tiled=True)


def shift(array, axis, step, size=4):
    return lax.ppermute(array, axis, [(i, (i + step) % size) for i in range(size)])


def both_ways(array, axis):
    return shift(array, axis, 1), shift(array, axis, 3)


def all_around(array, axis):
    return jnp.concatenate([array, *both_ways(array, axis), shift(array, axis, 2)])


def onward(from_low, from_high, axis):
    half = from_low.shape[1] // 2
    return shift(from_low[:, :half], axis, 1), shift(from_high[:, half:], axis, 3)


def combine(where, codes, psi, lefts, rights, first):
    width = psi.shape[-1]
    depth = sum(a.shape[1] for a in lefts[0])
    terms = depth // width
    count = len(lefts)
    left_parts = [a for group in lefts for a in group]
    right_parts = [a for group in rights for a in group]

    def place(i, where):
        source, k = i // count, i % count
        return where[source // 2], where[12] ^ (source % 2), where[4 + first + k], k

    def code_at(i, where):
        source, k = i // count, i % count
        return 128 * (first + k) + where[8 + source // 2] + (where[12] ^ (source % 2))

    def psi_at(i, where):
        g, c_r, x_j, _ = place(i, where)
        return (g * 4 + x_j) * 2 + c_r

    def out_index(i, where, codes):
        g, c_r, _, k = place(i, where)
        return (g * 2 + c_r) * count + k, 0, 0

    def kernel(where, codes, psi_ref, *refs):
        left_refs = refs[: len(left_parts)]
        right_refs = refs[len(left_parts) : len(left_parts) + len(right_parts)]
        out_ref, left_buf, right_buf, partial, left_sems, sems = refs[len(left_parts) + len(right_parts) :]
        i = pl.program_id(0)
        steps = pl.num_programs(0)

        def load_left(k, go):
            at = sum(len(group) for group in lefts[:k])
            row = 0
            for n, a in enumerate(lefts[k]):
                copy = pltpu.make_async_copy(
                    left_refs[at + n], left_buf.at[k, :, pl.ds(row, a.shape[1])], left_sems.at[k, n]
                )
                copy.start() if go else copy.wait()
                row += a.shape[1]

        def fetch(step, go):
            right = codes[code_at(step, where)] // 2
            slot = lax.rem(step, 2)
            at = 0
            for source, group in enumerate(rights):

                @pl.when(step // count == source)
                def _(at=at, group=group):
                    row = 0
                    for n, a in enumerate(group):
                        copy = pltpu.make_async_copy(
                            right_refs[at + n].at[right],
                            right_buf.at[slot, pl.ds(row, a.shape[1])],
                            sems.at[slot, n],
                        )
                        copy.start() if go else copy.wait()
                        row += a.shape[1]

                at += len(group)

        @pl.when(i == 0)
        def _():
            load_left(0, True)
            fetch(i, True)
            for k in range(1, count):
                load_left(k, True)

        @pl.when(i + 1 < steps)
        def _():
            fetch(i + 1, True)

        for k in range(count):

            @pl.when(i == k)
            def _(k=k):
                load_left(k, False)

        left = codes[code_at(i, where)] % 2
        k = lax.rem(i, count)
        for t in range(terms):
            block = left_buf[k, left, t * width : (t + 1) * width]
            product = jnp.dot(block, psi_ref[0], preferred_element_type=jnp.float32)
            partial[:, t * width : (t + 1) * width] = product.astype(BF16)
        fetch(i, False)
        total = jnp.dot(partial[...], right_buf[lax.rem(i, 2)], preferred_element_type=jnp.float32)
        out_ref[0] = total.astype(BF16)

    blocks = 2 * 4 * count
    parts = max(len(group) for group in rights + lefts)
    in_place = pl.BlockSpec(memory_space=pl.ANY)
    return pl.pallas_call(
        kernel,
        out_shape=jax.ShapeDtypeStruct((blocks, width, width), BF16),
        grid_spec=pltpu.PrefetchScalarGridSpec(
            num_scalar_prefetch=2,
            grid=(blocks,),
            in_specs=[pl.BlockSpec((1, width, width), lambda i, where, codes: (psi_at(i, where), 0, 0))]
            + [in_place] * (len(left_parts) + len(right_parts)),
            out_specs=pl.BlockSpec((1, width, width), out_index),
            scratch_shapes=[
                pltpu.VMEM((count, 2, depth, width), BF16),
                pltpu.VMEM((2, depth, width), BF16),
                pltpu.VMEM((width, depth), BF16),
                pltpu.SemaphoreType.DMA((count, parts)),
                pltpu.SemaphoreType.DMA((2, parts)),
            ],
        ),
        compiler_params=pltpu.CompilerParams(
            dimension_semantics=("arbitrary",), vmem_limit_bytes=VMEM
        ),
        cost_estimate=LONG if first else BRIEF,
        name=f"combine_{first}",
    )(where, codes, psi, *left_parts, *right_parts)


def assemble(where, pieces, applied=None):
    shape = pieces[0][2].shape
    kept = [] if applied is None else [applied]

    def kernel(where, *refs):
        piece_refs = refs[: len(pieces)]
        out_ref, sems = refs[len(pieces) + len(kept) :]
        copies = []
        for (first, count, _), ref in zip(pieces, piece_refs):
            size = 2 if count == 1 else 1
            for n in range(0, 8 * count, size):
                owner, k = n // count, n % count
                z_j, c_j = owner // 2, owner % 2
                to = z_j * 8 + where[4 + first + k] * 2 + c_j
                copies.append(
                    pltpu.make_async_copy(
                        ref.at[pl.ds(n, size)], out_ref.at[pl.ds(to, size)], sems.at[len(copies)]
                    )
                )
        for copy in copies:
            copy.start()
        for copy in copies:
            copy.wait()

    number = sum(4 if count == 1 else 8 * count for _, count, _ in pieces)
    in_place = pl.BlockSpec(memory_space=pltpu.HBM)
    return pl.pallas_call(
        kernel,
        out_shape=jax.ShapeDtypeStruct((32,) + shape[1:], BF16),
        grid_spec=pltpu.PrefetchScalarGridSpec(
            num_scalar_prefetch=1,
            grid=(1,),
            in_specs=[in_place] * (len(pieces) + len(kept)),
            out_specs=in_place,
            scratch_shapes=[pltpu.SemaphoreType.DMA((number,))],
        ),
        input_output_aliases={1 + len(pieces): 0} if kept else {},
        cost_estimate=BRIEF,
        compiler_params=pltpu.CompilerParams(vmem_limit_bytes=62 * 2**20),
        name=f"assemble_{len(kept)}",
    )(where, *[piece for _, _, piece in pieces], *kept)


def after(array, *others):
    return lax.optimization_barrier((array, *others))[0]


def body(where, wavefunction, pair_left, pair_right, left_env, left_dims, right_env, right_dims):
    width = wavefunction.shape[-1]
    sectors, terms = left_env.shape[:2]
    where = where.reshape(-1)

    psi = exchange(wavefunction, ("y", "x"))
    codes = all_around(all_around(pair_left + 2 * pair_right, "y"), "x")

    index = lax.broadcasted_iota(jnp.int32, right_env.shape, 2)
    right_own = jnp.where(index < right_dims[:, None, None, None], right_env, jnp.zeros_like(right_env))
    index = lax.broadcasted_iota(jnp.int32, left_env.shape, 3)
    left_own = jnp.where(index < left_dims[:, None, None, None], left_env, jnp.zeros_like(left_env))
    left_own = left_own.reshape(sectors, terms * width, width)
    right_own = right_own.reshape(sectors, terms * width, width)

    right_low, right_high = both_ways(right_own, "z")
    far = onward(*lax.optimization_barrier((right_low, right_high, psi))[:2], "z")
    rights = []
    for group in ((right_own,), (right_low,), (right_high,), far):
        rights.append(group)
        rights.append(tuple(shift(a, "c", 1, 2) for a in group))

    left_low, left_high = both_ways(after(left_own, psi), "x")
    left_far = onward(left_low, left_high, "x")

    def home(first, lefts):
        out = combine(where, codes, psi, lefts, rights, first)
        return first, len(lefts), exchange(out, ("z", "c"))

    own = home(0, [(left_own,)])
    near = home(1, [(left_low,), (left_high,)])
    opposite = home(3, [left_far])
    applied = assemble(where, [own, near])
    return assemble(where, [opposite], applied)


def solution(mesh):
    fine = Mesh(mesh.devices.reshape(4, 4, 4, 2), AXES)
    mapped = jax.shard_map(
        body, mesh=fine, in_specs=P(AXES), out_specs=P(AXES), check_vma=False
    )

    def run(*arrays):
        return mapped(jnp.asarray(ring_positions()), *arrays)

    return run
```

```python
import jax
import jax.numpy as jnp
import numpy as np
from jax import lax
from jax.experimental import pallas as pl
from jax.experimental.pallas import tpu as pltpu
from jax.sharding import Mesh, PartitionSpec as P

AXES = ("y", "z", "x", "c")
OFFSETS = (0, 3, 1, 2)
STEPS = (0, 1, 3, 2)
SLOTS = 3
BF16 = jnp.bfloat16
BRIEF = pl.CostEstimate(flops=1, bytes_accessed=1, transcendentals=0)
LONG = pl.CostEstimate(flops=10**12, bytes_accessed=1, transcendentals=0)
VMEM = 60 * 2**20


def ring_positions():
    rows = []
    for y, z, x, c in np.ndindex(4, 4, 4, 2):
        rows.append(
            [(z + o) % 4 for o in OFFSETS]
            + [(x + o) % 4 for o in OFFSETS]
            + [c]
            + [(x + o) % 4 for o in STEPS]
        )
    return np.asarray(rows, np.int32)


def exchange(array, axis):
    return lax.all_to_all(array, axis, split_axis=0, concat_axis=0, tiled=True)


def shift(array, axis, step, size=4):
    return lax.ppermute(array, axis, [(i, (i + step) % size) for i in range(size)])


def both_ways(array, axis):
    return shift(array, axis, 1), shift(array, axis, 3)


def onward(from_low, from_high, axis):
    half = from_low.shape[1] // 2
    return shift(from_low[:, :half], axis, 1), shift(from_high[:, half:], axis, 3)


def combine(where, codes, psi, lefts, rights, position):
    width = psi.shape[-1]
    depth = sum(a.shape[1] for a in lefts)
    terms = depth // width
    depth_of = SLOTS
    right_parts = [a for group in rights for a in group]

    def block_of(n, where):
        g, c_r = where[n // 2], where[8] ^ (n % 2)
        return g * 2 + c_r, (g * 4 + where[4 + position]) * 2 + c_r

    def kernel(where, codes, psi_ref, *refs):
        refs = list(refs)
        left_refs = [refs.pop(0) for _ in lefts]
        right_refs = [[refs.pop(0) for _ in group] for group in rights]
        out_ref, left_buf, right_buf, partial, left_sems, sems = refs
        step = pl.program_id(0)
        steps = pl.num_programs(0)

        def left_copies():
            row = 0
            for n, ref in enumerate(left_refs):
                size = ref.shape[1]
                yield pltpu.make_async_copy(ref, left_buf.at[:, pl.ds(row, size)], left_sems.at[n])
                row += size

        def fetch(at, go):
            slot = lax.rem(at, depth_of)
            for z_step in range(4):

                @pl.when(at == z_step)
                def _(z_step=z_step):
                    for core in range(2):
                        right = codes[block_of(2 * z_step + core, where)[1]] // 2
                        row = 0
                        for n, ref in enumerate(right_refs[2 * z_step + core]):
                            size = ref.shape[1]
                            copy = pltpu.make_async_copy(
                                ref.at[right],
                                right_buf.at[slot, core, pl.ds(row, size)],
                                sems.at[slot, core, n],
                            )
                            copy.start() if go else copy.wait()
                            row += size

        @pl.when(step == 0)
        def _():
            for copy in left_copies():
                copy.start()
            for ahead in range(depth_of - 1):
                fetch(ahead, True)

        @pl.when(step + depth_of - 1 < steps)
        def _():
            fetch(step + depth_of - 1, True)

        @pl.when(step == 0)
        def _():
            for copy in left_copies():
                copy.wait()

        fetch(step, False)
        slot = lax.rem(step, depth_of)
        for core in range(2):
            at, code_at = block_of(2 * step + core, where)
            left = codes[code_at] % 2
            block = psi_ref[at]
            for t in range(terms):
                product = jnp.dot(
                    left_buf[left, t * width : (t + 1) * width],
                    block,
                    preferred_element_type=jnp.float32,
                )
                partial[core, :, t * width : (t + 1) * width] = product.astype(BF16)
        for core in range(2):
            at, _ = block_of(2 * step + core, where)
            total = jnp.dot(partial[core], right_buf[slot, core], preferred_element_type=jnp.float32)
            out_ref[at] = total.astype(BF16)

    in_place = pl.BlockSpec(memory_space=pl.ANY)
    whole = lambda step, where, codes: (0, 0, 0)
    parts = max(len(group) for group in rights)
    return pl.pallas_call(
        kernel,
        out_shape=jax.ShapeDtypeStruct((8, width, width), BF16),
        grid_spec=pltpu.PrefetchScalarGridSpec(
            num_scalar_prefetch=2,
            grid=(4,),
            in_specs=[pl.BlockSpec((8, width, width), whole)]
            + [in_place] * (len(lefts) + len(right_parts)),
            out_specs=pl.BlockSpec((8, width, width), whole),
            scratch_shapes=[
                pltpu.VMEM((2, depth, width), BF16),
                pltpu.VMEM((depth_of, 2, depth, width), BF16),
                pltpu.VMEM((2, width, depth), BF16),
                pltpu.SemaphoreType.DMA((len(lefts),)),
                pltpu.SemaphoreType.DMA((depth_of, 2, parts)),
            ],
        ),
        compiler_params=pltpu.CompilerParams(
            dimension_semantics=("arbitrary",), vmem_limit_bytes=VMEM
        ),
        cost_estimate=LONG,
        name=f"combine_{position}",
    )(where, codes, psi, *lefts, *right_parts)


def assemble(where, pieces, applied=None):
    width = pieces[0][2].shape[-1]
    kept = [] if applied is None else [applied]
    steps = [(first + k, count, k) for first, count, _ in pieces for k in range(count)]

    def kernel(where, *refs):
        *piece_refs, out_ref = refs[: len(pieces)] + refs[-1:]
        p = pl.program_id(0)
        for n, ref in enumerate(r for (_, count, _), r in zip(pieces, piece_refs) for _ in range(count)):

            @pl.when(p == n)
            def _(ref=ref, k=steps[n][2]):
                out_ref[0, 0] = ref[0, :, k]

    def spec(count):
        return pl.BlockSpec((1, 2, count, width, width), lambda p, z_j, where: (z_j, 0, 0, 0, 0))

    def slot(p, z_j, where):
        return z_j, where[4 + pieces[0][0] + p], 0, 0, 0

    shaped = [piece.reshape(4, 2, count, width, width) for _, count, piece in pieces]
    return pl.pallas_call(
        kernel,
        out_shape=jax.ShapeDtypeStruct((4, 4, 2, width, width), BF16),
        grid_spec=pltpu.PrefetchScalarGridSpec(
            num_scalar_prefetch=1,
            grid=(len(steps), 4),
            in_specs=[spec(count) for _, count, _ in pieces]
            + [pl.BlockSpec(memory_space=pl.ANY)] * len(kept),
            out_specs=pl.BlockSpec((1, 1, 2, width, width), slot),
        ),
        input_output_aliases={1 + len(pieces): 0} if kept else {},
        compiler_params=pltpu.CompilerParams(vmem_limit_bytes=63 * 2**20 + 2**19),
        cost_estimate=BRIEF,
        name=f"assemble_{len(kept)}",
    )(where, *shaped, *kept)


def pick(where, psi, columns, cost):
    width = psi.shape[-1]

    def kernel(where, *refs):
        for n in range(len(columns)):
            refs[len(columns) + n][...] = refs[n][0, 0]

    def column(n):
        return pl.BlockSpec((1, 1, 2, width, width), lambda g, where: (g, where[9 + n], 0, 0, 0))

    return pl.pallas_call(
        kernel,
        out_shape=[jax.ShapeDtypeStruct((8, width, width), BF16)] * len(columns),
        grid_spec=pltpu.PrefetchScalarGridSpec(
            num_scalar_prefetch=1,
            grid=(4,),
            in_specs=[column(n) for n in columns],
            out_specs=[pl.BlockSpec((2, width, width), lambda g, where: (g, 0, 0))] * len(columns),
        ),
        compiler_params=pltpu.CompilerParams(vmem_limit_bytes=VMEM),
        cost_estimate=cost,
        name=f"pick_{columns[0]}",
    )(where, *[psi] * len(columns))


def together(*arrays):
    return lax.optimization_barrier(arrays)


def body(where, wavefunction, pair_left, pair_right, left_env, left_dims, right_env, right_dims):
    width = wavefunction.shape[-1]
    sectors, terms = left_env.shape[:2]
    where = where.reshape(-1)

    index = lax.broadcasted_iota(jnp.int32, right_env.shape, 2)
    right_own = jnp.where(index < right_dims[:, None, None, None], right_env, jnp.zeros_like(right_env))
    index = lax.broadcasted_iota(jnp.int32, left_env.shape, 3)
    left_own = jnp.where(index < left_dims[:, None, None, None], left_env, jnp.zeros_like(left_env))
    left_own = left_own.reshape(sectors, terms * width, width)
    right_own = right_own.reshape(sectors, terms * width, width)

    psi = exchange(wavefunction, "y").reshape(4, 4, 2, width, width)
    right_low, right_high = both_ways(right_own, "z")
    left_low, left_high = both_ways(left_own, "x")
    other_own = shift(right_own, "c", 1, 2)
    picks = pair_left + 2 * pair_right
    psi, right_low, right_high, left_low, left_high, other_own, picks = together(
        psi, right_low, right_high, left_low, left_high, other_own, picks
    )

    codes = exchange(picks, ("y", "x"))
    for_low, for_high = pick(where, psi, (1, 2), BRIEF)
    psi_own, psi_rest = pick(where, psi, (0, 3), LONG)
    psi_low, psi_high = shift(for_low, "x", 1), shift(for_high, "x", 3)
    far = onward(right_low, right_high, "z")
    others = [other_own, shift(right_low, "c", 1, 2), shift(right_high, "c", 1, 2)]
    psi_own, psi_rest, psi_low, psi_high, codes, others[1], others[2], *far = together(
        psi_own, psi_rest, psi_low, psi_high, codes, others[1], others[2], *far
    )

    left_far = onward(*together(left_low, left_high, psi_low)[:2], "x")
    psi_far = shift(psi_rest, "x", 2)
    rights = []
    for group, other in (
        ((right_own,), (others[0],)),
        ((right_low,), (others[1],)),
        ((right_high,), (others[2],)),
        (tuple(far), tuple(shift(a, "c", 1, 2) for a in far)),
    ):
        rights += [group, other]

    def home(position, psi, lefts):
        out = combine(where, codes, psi, lefts, rights, position)
        return position, 1, exchange(out, ("z", "c"))

    own = home(0, psi_own, (left_own,))
    low = home(1, psi_low, (left_low,))
    high = home(2, psi_high, (left_high,))
    applied = assemble(where, [own, low, high])
    rest = home(3, psi_far, left_far)
    return assemble(where, [rest], applied).reshape(wavefunction.shape)


def solution(mesh):
    fine = Mesh(mesh.devices.reshape(4, 4, 4, 2), AXES)
    mapped = jax.shard_map(
        body, mesh=fine, in_specs=P(AXES), out_specs=P(AXES), check_vma=False
    )

    def run(*arrays):
        return mapped(jnp.asarray(ring_positions()), *arrays)

    return run
```

```python
import jax
import jax.numpy as jnp
import numpy as np
from jax import lax
from jax.experimental import pallas as pl
from jax.experimental.pallas import tpu as pltpu
from jax.sharding import Mesh, PartitionSpec as P

AXES = ("y", "z", "x", "c")
OFFSETS = (0, 3, 1, 2)
STEPS = (0, 1, 3, 2)
SLOTS = 3
BF16 = jnp.bfloat16
BRIEF = pl.CostEstimate(flops=1, bytes_accessed=1, transcendentals=0)
LONG = pl.CostEstimate(flops=10**12, bytes_accessed=1, transcendentals=0)
VMEM = 60 * 2**20


def ring_positions():
    rows = []
    for y, z, x, c in np.ndindex(4, 4, 4, 2):
        rows.append(
            [(z + o) % 4 for o in OFFSETS]
            + [(x + o) % 4 for o in OFFSETS]
            + [c]
            + [(x + o) % 4 for o in STEPS]
        )
    return np.asarray(rows, np.int32)


def exchange(array, axis):
    return lax.all_to_all(array, axis, split_axis=0, concat_axis=0, tiled=True)


def shift(array, axis, step, size=4):
    return lax.ppermute(array, axis, [(i, (i + step) % size) for i in range(size)])


def both_ways(array, axis):
    return shift(array, axis, 1), shift(array, axis, 3)


def onward(from_low, from_high, axis):
    half = from_low.shape[1] // 2
    return shift(from_low[:, :half], axis, 1), shift(from_high[:, half:], axis, 3)


def combine(where, codes, psis, lefts, rights, first, z_first=0, kept=None):
    width = psis[0].shape[-1]
    depth = sum(a.shape[1] for a in lefts[0])
    terms = depth // width
    count = len(lefts)
    left_parts = [a for group in lefts for a in group]
    right_parts = [a for pair in rights for group in pair for a in group]
    steps = len(rights)
    slots = min(SLOTS, steps)
    each = [(core, k) for core in range(2) for k in range(count)]

    def code_of(step, core, k, where, codes):
        return codes[(where[z_first + step] * 4 + where[4 + first + k]) * 2 + (where[8] ^ core)]

    def kernel(where, codes, *refs):
        refs = list(refs)
        psi_refs = [refs.pop(0) for _ in psis]
        left_refs = [[refs.pop(0) for _ in group] for group in lefts]
        right_refs = [[[refs.pop(0) for _ in group] for group in pair] for pair in rights]
        out_ref, left_buf, right_buf, partial, left_sems, sems = refs[kept is not None :]
        step = pl.program_id(0)

        def copy_left(k, go):
            row = 0
            for n, ref in enumerate(left_refs[k]):
                size = ref.shape[1]
                copy = pltpu.make_async_copy(
                    ref, left_buf.at[k, :, pl.ds(row, size)], left_sems.at[k, n]
                )
                copy.start() if go else copy.wait()
                row += size

        def fetch(at, go):
            slot = lax.rem(at, slots)
            for n_step in range(steps):

                @pl.when(at == n_step)
                def _(n_step=n_step):
                    for n_block, (core, k) in enumerate(each):
                        right = code_of(n_step, core, k, where, codes) // 2
                        row = 0
                        for n, ref in enumerate(right_refs[n_step][core]):
                            size = ref.shape[1]
                            copy = pltpu.make_async_copy(
                                ref.at[right],
                                right_buf.at[slot, n_block, pl.ds(row, size)],
                                sems.at[slot, n_block, n],
                            )
                            copy.start() if go else copy.wait()
                            row += size

        @pl.when(step == 0)
        def _():
            for k in range(count):
                copy_left(k, True)
            for ahead in range(max(slots - 1, 1)):
                fetch(ahead, True)

        if slots > 1:

            @pl.when(step + slots - 1 < steps)
            def _():
                fetch(step + slots - 1, True)

        @pl.when(step == 0)
        def _():
            for k in range(count):
                copy_left(k, False)

        fetch(step, False)
        slot = lax.rem(step, slots)
        for n_block, (core, k) in enumerate(each):
            left = code_of(step, core, k, where, codes) % 2
            block = psi_refs[k][where[8] ^ core]
            for t in range(terms):
                product = jnp.dot(
                    left_buf[k, left, t * width : (t + 1) * width],
                    block,
                    preferred_element_type=jnp.float32,
                )
                partial[n_block, :, t * width : (t + 1) * width] = product.astype(BF16)
        for n_block, (core, k) in enumerate(each):
            total = jnp.dot(
                partial[n_block], right_buf[slot, n_block], preferred_element_type=jnp.float32
            )
            out_ref[(where[8] ^ core) * count + k] = total.astype(BF16)

    in_place = pl.BlockSpec(memory_space=pl.ANY)
    of_g = lambda step, where, codes: (where[z_first + step], 0, 0)
    parts = max(len(group) for pair in rights for group in pair)
    extra = [] if kept is None else [kept]
    operands = [*psis, *left_parts, *right_parts, *extra]
    return pl.pallas_call(
        kernel,
        out_shape=jax.ShapeDtypeStruct((8 * count, width, width), BF16),
        grid_spec=pltpu.PrefetchScalarGridSpec(
            num_scalar_prefetch=2,
            grid=(steps,),
            in_specs=[pl.BlockSpec((2, width, width), of_g)] * count
            + [in_place] * (len(operands) - count),
            out_specs=pl.BlockSpec((2 * count, width, width), of_g),
            scratch_shapes=[
                pltpu.VMEM((count, 2, depth, width), BF16),
                pltpu.VMEM((slots, len(each), depth, width), BF16),
                pltpu.VMEM((len(each), width, depth), BF16),
                pltpu.SemaphoreType.DMA((count, max(len(group) for group in lefts))),
                pltpu.SemaphoreType.DMA((slots, len(each), parts)),
            ],
        ),
        input_output_aliases={1 + len(operands): 0} if extra else {},
        compiler_params=pltpu.CompilerParams(
            dimension_semantics=("arbitrary",), vmem_limit_bytes=VMEM
        ),
        cost_estimate=LONG,
        name=f"combine_{first}_{z_first}",
    )(where, codes, *operands)


def assemble(where, pieces):
    width = pieces[0][1].shape[-1]
    counts = [piece.shape[0] // 8 for _, piece in pieces]

    def kernel(where, *refs):
        *piece_refs, out_ref = refs
        for (first, _), count, ref in zip(pieces, counts, piece_refs):
            for k in range(count):
                out_ref[0, where[4 + first + k]] = ref[0, :, k]

    at_z = lambda z_j, where: (z_j, 0, 0, 0, 0)
    return pl.pallas_call(
        kernel,
        out_shape=jax.ShapeDtypeStruct((4, 4, 2, width, width), BF16),
        grid_spec=pltpu.PrefetchScalarGridSpec(
            num_scalar_prefetch=1,
            grid=(4,),
            in_specs=[pl.BlockSpec((1, 2, count, width, width), at_z) for count in counts],
            out_specs=pl.BlockSpec((1, 4, 2, width, width), at_z),
        ),
        compiler_params=pltpu.CompilerParams(vmem_limit_bytes=VMEM),
        cost_estimate=BRIEF,
        name="assemble",
    )(where, *[p.reshape(4, 2, n, width, width) for (_, p), n in zip(pieces, counts)])


def pick(where, psi, columns, cost):
    width = psi.shape[-1]

    def kernel(where, *refs):
        for n in range(len(columns)):
            refs[len(columns) + n][...] = refs[n][0, 0]

    def column(n):
        return pl.BlockSpec((1, 1, 2, width, width), lambda g, where: (g, where[9 + n], 0, 0, 0))

    return pl.pallas_call(
        kernel,
        out_shape=[jax.ShapeDtypeStruct((8, width, width), BF16)] * len(columns),
        grid_spec=pltpu.PrefetchScalarGridSpec(
            num_scalar_prefetch=1,
            grid=(4,),
            in_specs=[column(n) for n in columns],
            out_specs=[pl.BlockSpec((2, width, width), lambda g, where: (g, 0, 0))] * len(columns),
        ),
        compiler_params=pltpu.CompilerParams(vmem_limit_bytes=VMEM),
        cost_estimate=cost,
        name=f"pick_{columns[0]}",
    )(where, *[psi] * len(columns))


def together(*arrays):
    return lax.optimization_barrier(arrays)


def body(where, wavefunction, pair_left, pair_right, left_env, left_dims, right_env, right_dims):
    width = wavefunction.shape[-1]
    sectors, terms = left_env.shape[:2]
    where = where.reshape(-1)

    index = lax.broadcasted_iota(jnp.int32, right_env.shape, 2)
    right_own = jnp.where(index < right_dims[:, None, None, None], right_env, jnp.zeros_like(right_env))
    index = lax.broadcasted_iota(jnp.int32, left_env.shape, 3)
    left_own = jnp.where(index < left_dims[:, None, None, None], left_env, jnp.zeros_like(left_env))
    left_own = left_own.reshape(sectors, terms * width, width)
    right_own = right_own.reshape(sectors, terms * width, width)

    psi = exchange(wavefunction, "y").reshape(4, 4, 2, width, width)
    right_low, right_high = both_ways(right_own, "z")
    left_low, left_high = both_ways(left_own, "x")
    other_own = shift(right_own, "c", 1, 2)
    picks = pair_left + 2 * pair_right
    psi, right_low, right_high, left_low, left_high, other_own, picks = together(
        psi, right_low, right_high, left_low, left_high, other_own, picks
    )

    for_low, for_high = pick(where, psi, (1, 2), BRIEF)
    far = onward(right_low, right_high, "z")
    for_low, for_high, psi, picks = together(for_low, for_high, psi, picks)
    psi_low, psi_high = shift(for_low, "x", 1), shift(for_high, "x", 3)
    codes = exchange(picks, ("y", "x"))
    psi_own, psi_rest = pick(where, psi, (0, 3), LONG)
    psi_rest, *to_core = together(psi_rest, right_low, right_high)
    other_low, other_high = [shift(a, "c", 1, 2) for a in to_core]
    rights = [
        ((right_own,), (other_own,)),
        ((right_low,), (other_low,)),
        ((right_high,), (other_high,)),
    ]
    left_own_ = (left_own,)
    own = combine(where, codes, [psi_own], [left_own_], rights, 0)
    halves = left_low[:, : terms * width // 2], left_high[:, terms * width // 2 :]
    psi_rest, psi_low, psi_high, own, *far_halves = together(
        psi_rest, psi_low, psi_high, own, *halves, *far
    )
    *halves, far_low, far_high = far_halves
    far = far_low, far_high

    left_far = shift(halves[0], "x", 1), shift(halves[1], "x", 3)
    psi_far = shift(psi_rest, "x", 2)
    rights.append((far, tuple(shift(a, "c", 1, 2) for a in far)))

    own = combine(where, codes, [psi_own], [left_own_], rights[3:], 0, 3, own)
    own = exchange(own, ("z", "c"))
    near = combine(where, codes, [psi_low, psi_high], [(left_low,), (left_high,)], rights, 1)
    near = exchange(near, ("z", "c"))
    rest = combine(where, codes, [psi_far], [left_far], rights, 3)
    rest = exchange(rest, ("z", "c"))
    applied = assemble(where, [(0, own), (1, near)])
    applied = lax.dynamic_update_slice(
        applied, rest.reshape(4, 1, 2, width, width), (0, where[7], 0, 0, 0)
    )
    return applied.reshape(wavefunction.shape)


def solution(mesh):
    fine = Mesh(mesh.devices.reshape(4, 4, 4, 2), AXES)
    mapped = jax.shard_map(
        body, mesh=fine, in_specs=P(AXES), out_specs=P(AXES), check_vma=False
    )

    def run(*arrays):
        return mapped(jnp.asarray(ring_positions()), *arrays)

    return run
```

```python
import jax
import jax.numpy as jnp
import numpy as np
from jax import lax
from jax.experimental import pallas as pl
from jax.experimental.pallas import tpu as pltpu
from jax.sharding import Mesh, PartitionSpec as P

AXES = ("y", "z", "x", "c")
OFFSETS = (0, 3, 1, 2)
STEPS = (0, 1, 3, 2)
SLOTS = 3
BF16 = jnp.bfloat16
BRIEF = pl.CostEstimate(flops=1, bytes_accessed=1, transcendentals=0)
LONG = pl.CostEstimate(flops=10**12, bytes_accessed=1, transcendentals=0)
VMEM = 60 * 2**20


def ring_positions():
    rows = []
    for y, z, x, c in np.ndindex(4, 4, 4, 2):
        rows.append(
            [(z + o) % 4 for o in OFFSETS]
            + [(x + o) % 4 for o in OFFSETS]
            + [c]
            + [(x + o) % 4 for o in STEPS]
        )
    return np.asarray(rows, np.int32)


def exchange(array, axis):
    return lax.all_to_all(array, axis, split_axis=0, concat_axis=0, tiled=True)


def shift(array, axis, step, size=4):
    return lax.ppermute(array, axis, [(i, (i + step) % size) for i in range(size)])


def both_ways(array, axis):
    return shift(array, axis, 1), shift(array, axis, 3)


def onward(from_low, from_high, axis):
    half = from_low.shape[1] // 2
    return shift(from_low[:, :half], axis, 1), shift(from_high[:, half:], axis, 3)


def combine(where, codes, psis, lefts, rights, first, z_first=0, kept=None):
    width = psis[0].shape[-1]
    depth = sum(a.shape[1] for a in lefts[0][0])
    terms = depth // width
    count = len(lefts)
    left_parts = [a for pair in lefts for group in pair for a in group]
    right_parts = [a for group in rights for a in group]
    steps = len(rights)
    slots = min(SLOTS, steps)
    each = [(core, k) for core in range(2) for k in range(count)]

    def code_of(step, core, k, where, codes):
        return codes[(where[z_first + step] * 4 + where[4 + first + k]) * 2 + (where[8] ^ core)]

    def kernel(where, codes, *refs):
        refs = list(refs)
        psi_refs = [refs.pop(0) for _ in psis]
        left_refs = [[[refs.pop(0) for _ in group] for group in pair] for pair in lefts]
        right_refs = [[refs.pop(0) for _ in group] for group in rights]
        out_ref, left_buf, right_buf, partial, left_sems, sems = refs[kept is not None :]
        step = pl.program_id(0)

        def copy_left(k, go):
            for core in range(2):
                row = 0
                for n, ref in enumerate(left_refs[k][core]):
                    size = ref.shape[1]
                    copy = pltpu.make_async_copy(
                        ref, left_buf.at[k, core, :, pl.ds(row, size)], left_sems.at[k, core, n]
                    )
                    copy.start() if go else copy.wait()
                    row += size

        def fetch(at, go):
            slot = lax.rem(at, slots)
            for n_step in range(steps):

                @pl.when(at == n_step)
                def _(n_step=n_step):
                    for n_block, (core, k) in enumerate(each):
                        right = code_of(n_step, core, k, where, codes) // 2
                        row = 0
                        for n, ref in enumerate(right_refs[n_step]):
                            size = ref.shape[1]
                            copy = pltpu.make_async_copy(
                                ref.at[right],
                                right_buf.at[slot, n_block, pl.ds(row, size)],
                                sems.at[slot, n_block, n],
                            )
                            copy.start() if go else copy.wait()
                            row += size

        @pl.when(step == 0)
        def _():
            for k in range(count):
                copy_left(k, True)
            for ahead in range(max(slots - 1, 1)):
                fetch(ahead, True)

        if slots > 1:

            @pl.when(step + slots - 1 < steps)
            def _():
                fetch(step + slots - 1, True)

        @pl.when(step == 0)
        def _():
            for k in range(count):
                copy_left(k, False)

        fetch(step, False)
        slot = lax.rem(step, slots)
        for n_block, (core, k) in enumerate(each):
            left = code_of(step, core, k, where, codes) % 2
            block = psi_refs[k][where[8] ^ core]
            for t in range(terms):
                product = jnp.dot(
                    left_buf[k, core, left, t * width : (t + 1) * width],
                    block,
                    preferred_element_type=jnp.float32,
                )
                partial[n_block, :, t * width : (t + 1) * width] = product.astype(BF16)
        for n_block, (core, k) in enumerate(each):
            total = jnp.dot(
                partial[n_block], right_buf[slot, n_block], preferred_element_type=jnp.float32
            )
            out_ref[(where[8] ^ core) * count + k] = total.astype(BF16)

    in_place = pl.BlockSpec(memory_space=pl.ANY)
    of_g = lambda step, where, codes: (where[z_first + step], 0, 0)
    parts = max(len(group) for group in rights)
    extra = [] if kept is None else [kept]
    operands = [*psis, *left_parts, *right_parts, *extra]
    return pl.pallas_call(
        kernel,
        out_shape=jax.ShapeDtypeStruct((8 * count, width, width), BF16),
        grid_spec=pltpu.PrefetchScalarGridSpec(
            num_scalar_prefetch=2,
            grid=(steps,),
            in_specs=[pl.BlockSpec((2, width, width), of_g)] * count
            + [in_place] * (len(operands) - count),
            out_specs=pl.BlockSpec((2 * count, width, width), of_g),
            scratch_shapes=[
                pltpu.VMEM((count, 2, 2, depth, width), BF16),
                pltpu.VMEM((slots, len(each), depth, width), BF16),
                pltpu.VMEM((len(each), width, depth), BF16),
                pltpu.SemaphoreType.DMA((count, 2, max(len(pair[0]) for pair in lefts))),
                pltpu.SemaphoreType.DMA((slots, len(each), parts)),
            ],
        ),
        input_output_aliases={1 + len(operands): 0} if extra else {},
        compiler_params=pltpu.CompilerParams(
            dimension_semantics=("arbitrary",), vmem_limit_bytes=VMEM
        ),
        cost_estimate=BRIEF if first == 3 else LONG,
        name=f"combine_{first}_{z_first}",
    )(where, codes, *operands)


def assemble(where, pieces):
    width = pieces[0][1].shape[-1]
    counts = [piece.shape[0] // 8 for _, piece in pieces]

    def kernel(where, *refs):
        *piece_refs, out_ref = refs
        for (first, _), count, ref in zip(pieces, counts, piece_refs):
            for k in range(count):
                out_ref[0, where[4 + first + k]] = ref[0, :, k]

    at_z = lambda z_j, where: (z_j, 0, 0, 0, 0)
    return pl.pallas_call(
        kernel,
        out_shape=jax.ShapeDtypeStruct((4, 4, 2, width, width), BF16),
        grid_spec=pltpu.PrefetchScalarGridSpec(
            num_scalar_prefetch=1,
            grid=(4,),
            in_specs=[pl.BlockSpec((1, 2, count, width, width), at_z) for count in counts],
            out_specs=pl.BlockSpec((1, 4, 2, width, width), at_z),
        ),
        compiler_params=pltpu.CompilerParams(vmem_limit_bytes=VMEM),
        cost_estimate=BRIEF,
        name="assemble",
    )(where, *[p.reshape(4, 2, n, width, width) for (_, p), n in zip(pieces, counts)])


def column(psi, position):
    zero = jnp.uint32(0)
    start = (zero, zero, position.astype(jnp.uint32), zero, zero)
    return lax.dynamic_slice(psi, start, (4, 2, 1) + psi.shape[3:]).reshape((8,) + psi.shape[3:])


def together(*arrays):
    return lax.optimization_barrier(arrays)


def body(where, wavefunction, pair_left, pair_right, left_env, left_dims, right_env, right_dims):
    width = wavefunction.shape[-1]
    sectors, terms = left_env.shape[:2]
    where = where.reshape(-1)

    index = lax.broadcasted_iota(jnp.int32, right_env.shape, 2)
    right_own = jnp.where(index < right_dims[:, None, None, None], right_env, jnp.zeros_like(right_env))
    index = lax.broadcasted_iota(jnp.int32, left_env.shape, 3)
    left_own = jnp.where(index < left_dims[:, None, None, None], left_env, jnp.zeros_like(left_env))
    left_own = left_own.reshape(sectors, terms * width, width)
    right_own = right_own.reshape(sectors, terms * width, width)

    codes = exchange(pair_left + 2 * pair_right, ("y", "x", "c"))
    psi = wavefunction.reshape(4, 4, 2, width, width).swapaxes(1, 2).reshape(wavefunction.shape)
    psi, codes = together(psi, codes)
    psi = exchange(psi, ("y", "c")).reshape(4, 2, 4, width, width)
    right_low, right_high = both_ways(right_own, "z")
    left_low, left_high = both_ways(left_own, "x")
    left_other = shift(left_own, "c", 1, 2)
    psi, right_low, right_high, left_low, left_high, left_other = together(
        psi, right_low, right_high, left_low, left_high, left_other
    )

    psi_low = shift(column(psi, where[10]), "x", 1)
    psi_high = shift(column(psi, where[11]), "x", 3)
    far = onward(right_low, right_high, "z")
    psi_own, psi_rest = column(psi, where[9]), column(psi, where[12])
    rights = [(right_own,), (right_low,), (right_high,)]
    lefts_own = [((left_own,), (left_other,))]
    own = combine(where, codes, [psi_own], lefts_own, rights, 0)
    own, left_low, left_high = together(own, left_low, left_high)
    halves = left_low[:, : terms * width // 2], left_high[:, terms * width // 2 :]
    psi_rest, psi_low, psi_high, own, *arrived = together(
        psi_rest, psi_low, psi_high, own, *halves, *far, left_low, left_high
    )
    *halves, far_low, far_high, left_low, left_high = arrived

    left_far = shift(halves[0], "x", 1), shift(halves[1], "x", 3)
    psi_far = shift(psi_rest, "x", 2)
    rights.append((far_low, far_high))
    own = combine(where, codes, [psi_own], lefts_own, rights[3:], 0, 3, own)
    own = exchange(own, "z")
    lefts_near = [((a,), (shift(a, "c", 1, 2),)) for a in (left_low, left_high)]
    near = combine(where, codes, [psi_low, psi_high], lefts_near, rights, 1)
    psi_far, *left_far = together(psi_far, *left_far, near)[:-1]
    near = exchange(near, "z")
    left_far = [(tuple(left_far), tuple(shift(a, "c", 1, 2) for a in left_far))]
    rest = combine(where, codes, [psi_far], left_far, rights, 3)
    rest = exchange(rest, "z")
    applied = assemble(where, [(0, own), (1, near)])
    zero = jnp.uint32(0)
    applied = lax.dynamic_update_slice(
        applied,
        rest.reshape(4, 1, 2, width, width),
        (zero, where[7].astype(jnp.uint32), zero, zero, zero),
    )
    return applied.reshape(wavefunction.shape)


def solution(mesh):
    fine = Mesh(mesh.devices.reshape(4, 4, 4, 2), AXES)
    mapped = jax.shard_map(
        body, mesh=fine, in_specs=P(AXES), out_specs=P(AXES), check_vma=False
    )

    def run(*arrays):
        return mapped(jnp.asarray(ring_positions()), *arrays)

    return run
```

```python
import jax
import jax.numpy as jnp
import numpy as np
from jax import lax
from jax.experimental import pallas as pl
from jax.experimental.pallas import tpu as pltpu
from jax.sharding import Mesh, PartitionSpec as P

AXES = ("y", "z", "x", "c")
OFFSETS = (0, 3, 1, 2)
STEPS = (0, 1, 3, 2)
TAIL = 16
SLOTS = 3
BF16 = jnp.bfloat16
BRIEF = pl.CostEstimate(flops=1, bytes_accessed=1, transcendentals=0)
LONG = pl.CostEstimate(flops=10**12, bytes_accessed=1, transcendentals=0)
VMEM = 60 * 2**20


def ring_positions():
    rows = []
    for y, z, x, c in np.ndindex(4, 4, 4, 2):
        rows.append(
            [(z + o) % 4 for o in OFFSETS]
            + [(x + o) % 4 for o in OFFSETS]
            + [c]
            + [(x + o) % 4 for o in STEPS]
        )
    return np.asarray(rows, np.int32)


def exchange(array, axis):
    return lax.all_to_all(array, axis, split_axis=0, concat_axis=0, tiled=True)


def shift(array, axis, step, size=4):
    return lax.ppermute(array, axis, [(i, (i + step) % size) for i in range(size)])


def both_ways(array, axis):
    return shift(array, axis, 1), shift(array, axis, 3)


def onward(from_low, from_high, axis):
    half = from_low.shape[1] // 2
    return shift(from_low[:, :half], axis, 1), shift(from_high[:, half:], axis, 3)


def combine(where, psis, lefts, rights, first, z_first=0, kept=None):
    codes = [codes for _, codes in psis]
    psis = [psi for psi, _ in psis]
    rows, width = psis[0].shape[1:]
    depth = sum(a.shape[1] for a in lefts[0][0])
    terms = depth // width
    count = len(lefts)
    left_parts = [a for pair in lefts for group in pair for a in group]
    right_parts = [a for group in rights for a in group]
    steps = len(rights)
    slots = min(SLOTS, steps)
    each = [(core, k) for core in range(2) for k in range(count)]

    def pick_of(step, core, k, side, where, codes):
        return codes[k][(where[z_first + step] * 2 + (where[8] ^ core)) * 2 + side]

    def kernel(where, *refs):
        codes, refs = refs[:count], list(refs[count:])
        psi_refs = [refs.pop(0) for _ in psis]
        left_refs = [[[refs.pop(0) for _ in group] for group in pair] for pair in lefts]
        right_refs = [[refs.pop(0) for _ in group] for group in rights]
        out_ref, left_buf, right_buf, partial, left_sems, sems = refs[kept is not None :]
        step = pl.program_id(0)

        def copy_left(k, go):
            for core in range(2):
                row = 0
                for n, ref in enumerate(left_refs[k][core]):
                    size = ref.shape[1]
                    copy = pltpu.make_async_copy(
                        ref, left_buf.at[k, core, :, pl.ds(row, size)], left_sems.at[k, core, n]
                    )
                    copy.start() if go else copy.wait()
                    row += size

        def fetch(at, go):
            slot = lax.rem(at, slots)
            for n_step in range(steps):

                @pl.when(at == n_step)
                def _(n_step=n_step):
                    for n_block, (core, k) in enumerate(each):
                        right = pick_of(n_step, core, k, 1, where, codes)
                        row = 0
                        for n, ref in enumerate(right_refs[n_step]):
                            size = ref.shape[1]
                            copy = pltpu.make_async_copy(
                                ref.at[right],
                                right_buf.at[slot, n_block, pl.ds(row, size)],
                                sems.at[slot, n_block, n],
                            )
                            copy.start() if go else copy.wait()
                            row += size

        @pl.when(step == 0)
        def _():
            for k in range(count):
                copy_left(k, True)
            for ahead in range(max(slots - 1, 1)):
                fetch(ahead, True)

        if slots > 1:

            @pl.when(step + slots - 1 < steps)
            def _():
                fetch(step + slots - 1, True)

        @pl.when(step == 0)
        def _():
            for k in range(count):
                copy_left(k, False)

        fetch(step, False)
        slot = lax.rem(step, slots)
        for n_block, (core, k) in enumerate(each):
            left = pick_of(step, core, k, 0, where, codes)
            block = psi_refs[k][where[8] ^ core, :width]
            for t in range(terms):
                product = jnp.dot(
                    left_buf[k, core, left, t * width : (t + 1) * width],
                    block,
                    preferred_element_type=jnp.float32,
                )
                partial[n_block, :, t * width : (t + 1) * width] = product.astype(BF16)
        for n_block, (core, k) in enumerate(each):
            total = jnp.dot(
                partial[n_block], right_buf[slot, n_block], preferred_element_type=jnp.float32
            )
            out_ref[(where[8] ^ core) * count + k] = total.astype(BF16)

    in_place = pl.BlockSpec(memory_space=pl.ANY)
    of_g = lambda step, where, *codes: (where[z_first + step], 0, 0)
    parts = max(len(group) for group in rights)
    extra = [] if kept is None else [kept]
    operands = [*psis, *left_parts, *right_parts, *extra]
    return pl.pallas_call(
        kernel,
        out_shape=jax.ShapeDtypeStruct((8 * count, width, width), BF16),
        grid_spec=pltpu.PrefetchScalarGridSpec(
            num_scalar_prefetch=1 + count,
            grid=(steps,),
            in_specs=[pl.BlockSpec((2, rows, width), of_g)] * count
            + [in_place] * (len(operands) - count),
            out_specs=pl.BlockSpec((2 * count, width, width), of_g),
            scratch_shapes=[
                pltpu.VMEM((count, 2, 2, depth, width), BF16),
                pltpu.VMEM((slots, len(each), depth, width), BF16),
                pltpu.VMEM((len(each), width, depth), BF16),
                pltpu.SemaphoreType.DMA((count, 2, max(len(pair[0]) for pair in lefts))),
                pltpu.SemaphoreType.DMA((slots, len(each), parts)),
            ],
        ),
        input_output_aliases={count + len(operands): 0} if extra else {},
        compiler_params=pltpu.CompilerParams(
            dimension_semantics=("arbitrary",), vmem_limit_bytes=VMEM
        ),
        cost_estimate=BRIEF if first == 3 or z_first else LONG,
        name=f"combine_{first}_{z_first}",
    )(where, *codes, *operands)


def assemble(where, pieces):
    width = pieces[0][1].shape[-1]
    counts = [piece.shape[0] // 8 for _, piece in pieces]

    def kernel(where, *refs):
        *piece_refs, out_ref = refs
        for (first, _), count, ref in zip(pieces, counts, piece_refs):
            for k in range(count):
                out_ref[0, where[4 + first + k]] = ref[0, :, k]

    at_z = lambda z_j, where: (z_j, 0, 0, 0, 0)
    return pl.pallas_call(
        kernel,
        out_shape=jax.ShapeDtypeStruct((4, 4, 2, width, width), BF16),
        grid_spec=pltpu.PrefetchScalarGridSpec(
            num_scalar_prefetch=1,
            grid=(4,),
            in_specs=[pl.BlockSpec((1, 2, count, width, width), at_z) for count in counts],
            out_specs=pl.BlockSpec((1, 4, 2, width, width), at_z),
        ),
        compiler_params=pltpu.CompilerParams(vmem_limit_bytes=VMEM),
        cost_estimate=BRIEF,
        name="assemble",
    )(where, *[p.reshape(4, 2, n, width, width) for (_, p), n in zip(pieces, counts)])


def pack(wavefunction, pair_left, pair_right):
    width = wavefunction.shape[-1]

    def kernel(left, right, in_ref, out_ref):
        lane = lax.broadcasted_iota(jnp.int32, (TAIL, width), 1)
        for x_r, c_r in np.ndindex(4, 2):
            slot = x_r * 2 + c_r
            n = pl.program_id(0) * 8 + slot
            picks = jnp.where(lane == 0, left[n], jnp.where(lane == 1, right[n], 0))
            out_ref[c_r, x_r, :width] = in_ref[slot]
            out_ref[c_r, x_r, width:] = picks.astype(jnp.float32).astype(BF16)

    return pl.pallas_call(
        kernel,
        out_shape=jax.ShapeDtypeStruct((8, 4, width + TAIL, width), BF16),
        grid_spec=pltpu.PrefetchScalarGridSpec(
            num_scalar_prefetch=2,
            grid=(4,),
            in_specs=[pl.BlockSpec((8, width, width), lambda q, left, right: (q, 0, 0))],
            out_specs=pl.BlockSpec((2, 4, width + TAIL, width), lambda q, left, right: (q, 0, 0, 0)),
        ),
        compiler_params=pltpu.CompilerParams(vmem_limit_bytes=VMEM),
        cost_estimate=BRIEF,
        name="pack",
    )(pair_left, pair_right, wavefunction)


def column(psi, position):
    zero = jnp.uint32(0)
    start = (zero, position.astype(jnp.uint32), zero, zero)
    return lax.dynamic_slice(psi, start, (8, 1) + psi.shape[2:]).reshape((8,) + psi.shape[2:])


def split(piece):
    return piece, piece[:, -TAIL, :2].astype(jnp.int32).reshape(-1)


def together(*arrays):
    return lax.optimization_barrier(arrays)


def body(where, wavefunction, pair_left, pair_right, left_env, left_dims, right_env, right_dims):
    width = wavefunction.shape[-1]
    sectors, terms = left_env.shape[:2]
    where = where.reshape(-1)

    index = lax.broadcasted_iota(jnp.int32, right_env.shape, 2)
    right_own = jnp.where(index < right_dims[:, None, None, None], right_env, jnp.zeros_like(right_env))
    index = lax.broadcasted_iota(jnp.int32, left_env.shape, 3)
    left_own = jnp.where(index < left_dims[:, None, None, None], left_env, jnp.zeros_like(left_env))
    left_own = left_own.reshape(sectors, terms * width, width)
    right_own = right_own.reshape(sectors, terms * width, width)

    psi = exchange(pack(wavefunction, pair_left, pair_right), ("y", "c"))
    right_low, right_high = both_ways(right_own, "z")
    left_low, left_high = both_ways(left_own, "x")
    left_other = shift(left_own, "c", 1, 2)
    psi, right_low, right_high, left_low, left_high, left_other = together(
        psi, right_low, right_high, left_low, left_high, left_other
    )

    for_low, for_high = column(psi, where[10]), column(psi, where[11])
    for_low, for_high, psi, *to_far = together(for_low, for_high, psi, right_low, right_high)
    psi_low, psi_high = shift(for_low, "x", 1), shift(for_high, "x", 3)
    far = onward(*to_far, "z")
    psi_own, psi_rest = split(column(psi, where[9])), column(psi, where[12])
    rights = [(right_own,), (right_low,), (right_high,)]
    lefts_own = [((left_own,), (left_other,))]
    own = combine(where, [psi_own], lefts_own, rights, 0)
    own, left_low, left_high = together(own, left_low, left_high)
    halves = left_low[:, : terms * width // 2], left_high[:, terms * width // 2 :]
    rights.append(tuple(far))
    own = combine(where, [psi_own], lefts_own, rights[3:], 0, 3, own)
    psi_rest, psi_low, psi_high, own, left_low, left_high, *halves = together(
        psi_rest, psi_low, psi_high, own, left_low, left_high, *halves
    )

    left_far = shift(halves[0], "x", 1), shift(halves[1], "x", 3)
    psi_far = shift(psi_rest, "x", 2)
    own = exchange(own, "z")
    lefts_near = [((a,), (shift(a, "c", 1, 2),)) for a in (left_low, left_high)]
    near = combine(where, [split(psi_low), split(psi_high)], lefts_near, rights, 1)
    left_far = together(*left_far, near)[:-1]
    near = exchange(near, "z")
    left_far = [(tuple(left_far), tuple(shift(a, "c", 1, 2) for a in left_far))]
    rest = combine(where, [split(psi_far)], left_far, rights, 3)
    rest = exchange(rest, "z")
    applied = assemble(where, [(0, own), (1, near)])
    zero = jnp.uint32(0)
    applied = lax.dynamic_update_slice(
        applied,
        rest.reshape(4, 1, 2, width, width),
        (zero, where[7].astype(jnp.uint32), zero, zero, zero),
    )
    return applied.reshape(wavefunction.shape)


def solution(mesh):
    fine = Mesh(mesh.devices.reshape(4, 4, 4, 2), AXES)
    mapped = jax.shard_map(
        body, mesh=fine, in_specs=P(AXES), out_specs=P(AXES), check_vma=False
    )

    def run(*arrays):
        return mapped(jnp.asarray(ring_positions()), *arrays)

    return run
```

```python
import jax
import jax.numpy as jnp
import numpy as np
from jax import lax
from jax.experimental import pallas as pl
from jax.experimental.pallas import tpu as pltpu
from jax.sharding import Mesh, PartitionSpec as P

AXES = ("y", "z", "x", "c")
OFFSETS = (0, 3, 1, 2)
STEPS = (0, 1, 3, 2)
TAIL = 16
SLOTS = 3
BF16 = jnp.bfloat16
BRIEF = pl.CostEstimate(flops=1, bytes_accessed=1, transcendentals=0)
LONG = pl.CostEstimate(flops=10**12, bytes_accessed=1, transcendentals=0)
VMEM = 60 * 2**20


def ring_positions():
    rows = []
    for y, z, x, c in np.ndindex(4, 4, 4, 2):
        rows.append(
            [(z + o) % 4 for o in OFFSETS]
            + [(x + o) % 4 for o in OFFSETS]
            + [c]
            + [(x + o) % 4 for o in STEPS]
        )
    return np.asarray(rows, np.int32)


def exchange(array, axis):
    return lax.all_to_all(array, axis, split_axis=0, concat_axis=0, tiled=True)


def shift(array, axis, step, size=4):
    return lax.ppermute(array, axis, [(i, (i + step) % size) for i in range(size)])


def both_ways(array, axis):
    return shift(array, axis, 1), shift(array, axis, 3)


def onward(from_low, from_high, axis):
    half = from_low.shape[1] // 2
    return shift(from_low[:, :half], axis, 1), shift(from_high[:, half:], axis, 3)


def combine(where, psis, lefts, rights, first, z_first=0, kept=None):
    codes = [codes for _, codes in psis]
    psis = [psi for psi, _ in psis]
    rows, width = psis[0].shape[2:]
    columns = psis[0].shape[1]
    depth = sum(a.shape[1] for a in lefts[0][0])
    terms = depth // width
    count = len(lefts)
    left_parts = [a for pair in lefts for group in pair for a in group]
    right_parts = [a for group in rights for a in group]
    steps = len(rights)
    slots = min(SLOTS, steps)
    each = [(core, k) for core in range(2) for k in range(count)]

    def mine(where):
        return where[9] if columns > 1 else 0

    def pick_of(step, core, k, side, where, codes):
        block = where[z_first + step] * 2 + (where[8] ^ core)
        return codes[k][(block * columns + mine(where)) * 2 + side]

    def kernel(where, *refs):
        codes, refs = refs[:count], list(refs[count:])
        psi_refs = [refs.pop(0) for _ in psis]
        left_refs = [[[refs.pop(0) for _ in group] for group in pair] for pair in lefts]
        right_refs = [[refs.pop(0) for _ in group] for group in rights]
        out_ref, left_buf, right_buf, partial, left_sems, sems = refs[kept is not None :]
        step = pl.program_id(0)

        def copy_left(k, go):
            for core in range(2):
                row = 0
                for n, ref in enumerate(left_refs[k][core]):
                    size = ref.shape[1]
                    copy = pltpu.make_async_copy(
                        ref, left_buf.at[k, core, :, pl.ds(row, size)], left_sems.at[k, core, n]
                    )
                    copy.start() if go else copy.wait()
                    row += size

        def fetch(at, go):
            slot = lax.rem(at, slots)
            for n_step in range(steps):

                @pl.when(at == n_step)
                def _(n_step=n_step):
                    for n_block, (core, k) in enumerate(each):
                        right = pick_of(n_step, core, k, 1, where, codes)
                        row = 0
                        for n, ref in enumerate(right_refs[n_step]):
                            size = ref.shape[1]
                            copy = pltpu.make_async_copy(
                                ref.at[right],
                                right_buf.at[slot, n_block, pl.ds(row, size)],
                                sems.at[slot, n_block, n],
                            )
                            copy.start() if go else copy.wait()
                            row += size

        @pl.when(step == 0)
        def _():
            for k in range(count):
                copy_left(k, True)
            for ahead in range(max(slots - 1, 1)):
                fetch(ahead, True)

        if slots > 1:

            @pl.when(step + slots - 1 < steps)
            def _():
                fetch(step + slots - 1, True)

        @pl.when(step == 0)
        def _():
            for k in range(count):
                copy_left(k, False)

        fetch(step, False)
        slot = lax.rem(step, slots)
        for n_block, (core, k) in enumerate(each):
            left = pick_of(step, core, k, 0, where, codes)
            block = psi_refs[k][where[8] ^ core, 0, :width]
            for t in range(terms):
                product = jnp.dot(
                    left_buf[k, core, left, t * width : (t + 1) * width],
                    block,
                    preferred_element_type=jnp.float32,
                )
                partial[n_block, :, t * width : (t + 1) * width] = product.astype(BF16)
        for n_block, (core, k) in enumerate(each):
            total = jnp.dot(
                partial[n_block], right_buf[slot, n_block], preferred_element_type=jnp.float32
            )
            out_ref[(where[8] ^ core) * count + k] = total.astype(BF16)

    in_place = pl.BlockSpec(memory_space=pl.ANY)
    of_g = lambda step, where, *codes: (where[z_first + step], 0, 0)
    psi_of_g = lambda step, where, *codes: (where[z_first + step], mine(where), 0, 0)
    parts = max(len(group) for group in rights)
    extra = [] if kept is None else [kept]
    operands = [*psis, *left_parts, *right_parts, *extra]
    return pl.pallas_call(
        kernel,
        out_shape=jax.ShapeDtypeStruct((8 * count, width, width), BF16),
        grid_spec=pltpu.PrefetchScalarGridSpec(
            num_scalar_prefetch=1 + count,
            grid=(steps,),
            in_specs=[pl.BlockSpec((2, 1, rows, width), psi_of_g)] * count
            + [in_place] * (len(operands) - count),
            out_specs=pl.BlockSpec((2 * count, width, width), of_g),
            scratch_shapes=[
                pltpu.VMEM((count, 2, 2, depth, width), BF16),
                pltpu.VMEM((slots, len(each), depth, width), BF16),
                pltpu.VMEM((len(each), width, depth), BF16),
                pltpu.SemaphoreType.DMA((count, 2, max(len(pair[0]) for pair in lefts))),
                pltpu.SemaphoreType.DMA((slots, len(each), parts)),
            ],
        ),
        input_output_aliases={count + len(operands): 0} if extra else {},
        compiler_params=pltpu.CompilerParams(
            dimension_semantics=("arbitrary",), vmem_limit_bytes=VMEM
        ),
        cost_estimate=BRIEF if first == 3 or z_first else LONG,
        name=f"combine_{first}_{z_first}",
    )(where, *codes, *operands)


def assemble(where, pieces):
    width = pieces[0][1].shape[-1]
    counts = [piece.shape[0] // 8 for _, piece in pieces]

    def kernel(where, *refs):
        *piece_refs, out_ref = refs
        for (first, _), count, ref in zip(pieces, counts, piece_refs):
            for k in range(count):
                out_ref[0, where[4 + first + k]] = ref[0, :, k]

    at_z = lambda z_j, where: (z_j, 0, 0, 0, 0)
    return pl.pallas_call(
        kernel,
        out_shape=jax.ShapeDtypeStruct((4, 4, 2, width, width), BF16),
        grid_spec=pltpu.PrefetchScalarGridSpec(
            num_scalar_prefetch=1,
            grid=(4,),
            in_specs=[pl.BlockSpec((1, 2, count, width, width), at_z) for count in counts],
            out_specs=pl.BlockSpec((1, 4, 2, width, width), at_z),
        ),
        compiler_params=pltpu.CompilerParams(vmem_limit_bytes=VMEM),
        cost_estimate=BRIEF,
        name="assemble",
    )(where, *[p.reshape(4, 2, n, width, width) for (_, p), n in zip(pieces, counts)])


def pack(wavefunction, pair_left, pair_right):
    width = wavefunction.shape[-1]

    def kernel(left, right, in_ref, out_ref):
        lane = lax.broadcasted_iota(jnp.int32, (TAIL, width), 1)
        for x_r, c_r in np.ndindex(4, 2):
            slot = x_r * 2 + c_r
            n = pl.program_id(0) * 8 + slot
            picks = jnp.where(lane == 0, left[n], jnp.where(lane == 1, right[n], 0))
            out_ref[c_r, x_r, :width] = in_ref[slot]
            out_ref[c_r, x_r, width:] = picks.astype(jnp.float32).astype(BF16)

    return pl.pallas_call(
        kernel,
        out_shape=jax.ShapeDtypeStruct((8, 4, width + TAIL, width), BF16),
        grid_spec=pltpu.PrefetchScalarGridSpec(
            num_scalar_prefetch=2,
            grid=(4,),
            in_specs=[pl.BlockSpec((8, width, width), lambda q, left, right: (q, 0, 0))],
            out_specs=pl.BlockSpec((2, 4, width + TAIL, width), lambda q, left, right: (q, 0, 0, 0)),
        ),
        compiler_params=pltpu.CompilerParams(vmem_limit_bytes=VMEM),
        cost_estimate=BRIEF,
        name="pack",
    )(pair_left, pair_right, wavefunction)


def column(psi, position):
    zero = jnp.uint32(0)
    start = (zero, position.astype(jnp.uint32), zero, zero)
    return lax.dynamic_slice(psi, start, (8, 1) + psi.shape[2:])


def split(piece):
    return piece, piece[:, :, -TAIL, :2].astype(jnp.int32).reshape(-1)


def together(*arrays):
    return lax.optimization_barrier(arrays)


def body(where, wavefunction, pair_left, pair_right, left_env, left_dims, right_env, right_dims):
    width = wavefunction.shape[-1]
    sectors, terms = left_env.shape[:2]
    where = where.reshape(-1)

    index = lax.broadcasted_iota(jnp.int32, right_env.shape, 2)
    right_own = jnp.where(index < right_dims[:, None, None, None], right_env, jnp.zeros_like(right_env))
    index = lax.broadcasted_iota(jnp.int32, left_env.shape, 3)
    left_own = jnp.where(index < left_dims[:, None, None, None], left_env, jnp.zeros_like(left_env))
    left_own = left_own.reshape(sectors, terms * width, width)
    right_own = right_own.reshape(sectors, terms * width, width)

    psi = exchange(pack(wavefunction, pair_left, pair_right), ("y", "c"))
    right_low, right_high = both_ways(right_own, "z")
    left_low, left_high = both_ways(left_own, "x")
    left_other = shift(left_own, "c", 1, 2)
    psi, right_low, right_high, left_low, left_high, left_other = together(
        psi, right_low, right_high, left_low, left_high, left_other
    )

    for_low, for_high = column(psi, where[10]), column(psi, where[11])
    for_low, for_high, psi, *to_far = together(for_low, for_high, psi, right_low, right_high)
    psi_low, psi_high = shift(for_low, "x", 1), shift(for_high, "x", 3)
    far = onward(*to_far, "z")
    psi_own = split(psi)
    rights = [(right_own,), (right_low,), (right_high,)]
    lefts_own = [((left_own,), (left_other,))]
    own = combine(where, [psi_own], lefts_own, rights, 0)
    own, psi, left_low, left_high = together(own, psi, left_low, left_high)
    halves = left_low[:, : terms * width // 2], left_high[:, terms * width // 2 :]
    rights.append(tuple(far))
    own = combine(where, [psi_own], lefts_own, rights[3:], 0, 3, own)
    psi_rest, psi_low, psi_high, own, left_low, left_high, *halves = together(
        column(psi, where[12]), psi_low, psi_high, own, left_low, left_high, *halves
    )

    left_far = shift(halves[0], "x", 1), shift(halves[1], "x", 3)
    psi_far = shift(psi_rest, "x", 2)
    own = exchange(own, "z")
    others = [shift(a, "c", 1, 2) for a in (left_low, left_high)]
    psi_low, psi_high, *others = together(psi_low, psi_high, *others)
    lefts_near = [((left_low,), (others[0],)), ((left_high,), (others[1],))]
    near = combine(where, [split(psi_low), split(psi_high)], lefts_near, rights, 1)
    psi_far, *left_far = together(psi_far, *left_far, near)[:-1]
    near = exchange(near, "z")
    left_far = [(tuple(left_far), tuple(shift(a, "c", 1, 2) for a in left_far))]
    rest = combine(where, [split(psi_far)], left_far, rights, 3)
    rest = exchange(rest, "z")
    applied = assemble(where, [(0, own), (1, near)])
    zero = jnp.uint32(0)
    applied = lax.dynamic_update_slice(
        applied,
        rest.reshape(4, 1, 2, width, width),
        (zero, where[7].astype(jnp.uint32), zero, zero, zero),
    )
    return applied.reshape(wavefunction.shape)


def solution(mesh):
    fine = Mesh(mesh.devices.reshape(4, 4, 4, 2), AXES)
    mapped = jax.shard_map(
        body, mesh=fine, in_specs=P(AXES), out_specs=P(AXES), check_vma=False
    )

    def run(*arrays):
        return mapped(jnp.asarray(ring_positions()), *arrays)

    return run
```

```python
import jax
import jax.numpy as jnp
import numpy as np
from jax import lax
from jax.experimental import pallas as pl
from jax.experimental.pallas import tpu as pltpu
from jax.sharding import Mesh, PartitionSpec as P

AXES = ("y", "z", "x", "c")
OFFSETS = (0, 3, 1, 2)
STEPS = (0, 1, 3, 2)
TAIL = 16
SLOTS = 3
BF16 = jnp.bfloat16
BRIEF = pl.CostEstimate(flops=1, bytes_accessed=1, transcendentals=0)
LONG = pl.CostEstimate(flops=10**12, bytes_accessed=1, transcendentals=0)
VMEM = 60 * 2**20


def ring_positions():
    rows = []
    for y, z, x, c in np.ndindex(4, 4, 4, 2):
        rows.append(
            [(z + o) % 4 for o in OFFSETS]
            + [(x + o) % 4 for o in OFFSETS]
            + [c]
            + [(x + o) % 4 for o in STEPS]
        )
    return np.asarray(rows, np.int32)


def exchange(array, axis):
    return lax.all_to_all(array, axis, split_axis=0, concat_axis=0, tiled=True)


def shift(array, axis, step, size=4):
    return lax.ppermute(array, axis, [(i, (i + step) % size) for i in range(size)])


def both_ways(array, axis):
    return shift(array, axis, 1), shift(array, axis, 3)


def onward(from_low, from_high, axis):
    half = from_low.shape[1] // 2
    return shift(from_low[:, :half], axis, 1), shift(from_high[:, half:], axis, 3)


def combine(where, psis, lefts, rights, first, z_first=0, kept=None, cores=(0, 1)):
    codes = [codes for _, codes in psis]
    psis = [psi for psi, _ in psis]
    rows, width = psis[0].shape[2:]
    columns = psis[0].shape[1]
    depth = sum(a.shape[1] for a in lefts[0][0])
    terms = depth // width
    count = len(lefts)
    left_parts = [a for pair in lefts for group in pair for a in group]
    right_parts = [a for group in rights for a in group]
    steps = len(rights)
    slots = min(SLOTS, steps)
    each = [(core, k) for core in cores for k in range(count)]

    def mine(where):
        return where[9] if columns > 1 else 0

    def pick_of(step, core, k, side, where, codes):
        block = where[z_first + step] * 2 + (where[8] ^ core)
        return codes[k][(block * columns + mine(where)) * 2 + side]

    def kernel(where, *refs):
        codes, refs = refs[:count], list(refs[count:])
        psi_refs = [refs.pop(0) for _ in psis]
        left_refs = [[[refs.pop(0) for _ in group] for group in pair] for pair in lefts]
        right_refs = [[refs.pop(0) for _ in group] for group in rights]
        out_ref, left_buf, right_buf, partial, left_sems, sems = refs[kept is not None :]
        step = pl.program_id(0)

        def copy_lefts(needed, go):
            for core, k in each:
                at = core - cores[0]
                pick = pick_of(0, core, k, 0, where, codes)
                pick = pick if needed else 1 - pick
                row = 0
                for n, ref in enumerate(left_refs[k][at]):
                    size = ref.shape[1]
                    copy = pltpu.make_async_copy(
                        ref.at[pick],
                        left_buf.at[k, at, pick, pl.ds(row, size)],
                        left_sems.at[k, at, n, 0 if needed else 1],
                    )
                    copy.start() if go else copy.wait()
                    row += size

        def fetch(at, go):
            slot = lax.rem(at, slots)
            for n_step in range(steps):

                @pl.when(at == n_step)
                def _(n_step=n_step):
                    for n_block, (core, k) in enumerate(each):
                        right = pick_of(n_step, core, k, 1, where, codes)
                        row = 0
                        for n, ref in enumerate(right_refs[n_step]):
                            size = ref.shape[1]
                            copy = pltpu.make_async_copy(
                                ref.at[right],
                                right_buf.at[slot, n_block, pl.ds(row, size)],
                                sems.at[slot, n_block, n],
                            )
                            copy.start() if go else copy.wait()
                            row += size

        @pl.when(step == 0)
        def _():
            copy_lefts(True, True)
            fetch(0, True)
            if steps > 1:
                copy_lefts(False, True)
            for ahead in range(1, slots - 1):
                fetch(ahead, True)

        if slots > 1:

            @pl.when(step + slots - 1 < steps)
            def _():
                fetch(step + slots - 1, True)

        @pl.when(step == 0)
        def _():
            copy_lefts(True, False)

        if steps > 1:

            @pl.when(step == 1)
            def _():
                copy_lefts(False, False)

        fetch(step, False)
        slot = lax.rem(step, slots)
        for n_block, (core, k) in enumerate(each):
            left = pick_of(step, core, k, 0, where, codes)
            block = psi_refs[k][where[8] ^ core, 0, :width]
            for t in range(terms):
                product = jnp.dot(
                    left_buf[k, core - cores[0], left, t * width : (t + 1) * width],
                    block,
                    preferred_element_type=jnp.float32,
                )
                partial[n_block, :, t * width : (t + 1) * width] = product.astype(BF16)
        for n_block, (core, k) in enumerate(each):
            total = jnp.dot(
                partial[n_block], right_buf[slot, n_block], preferred_element_type=jnp.float32
            )
            row = (where[8] ^ core) * count if len(cores) > 1 else 0
            out_ref[row + k] = total.astype(BF16)

    in_place = pl.BlockSpec(memory_space=pl.ANY)

    def of_g(step, where, *codes):
        g = where[z_first + step]
        return (g if len(cores) > 1 else g * 2 + (where[8] ^ cores[0])), 0, 0

    psi_of_g = lambda step, where, *codes: (where[z_first + step], mine(where), 0, 0)
    parts = max(len(group) for group in rights)
    extra = [] if kept is None else [kept]
    operands = [*psis, *left_parts, *right_parts, *extra]
    return pl.pallas_call(
        kernel,
        out_shape=jax.ShapeDtypeStruct((8 * count, width, width), BF16),
        grid_spec=pltpu.PrefetchScalarGridSpec(
            num_scalar_prefetch=1 + count,
            grid=(steps,),
            in_specs=[pl.BlockSpec((2, 1, rows, width), psi_of_g)] * count
            + [in_place] * (len(operands) - count),
            out_specs=pl.BlockSpec((len(cores) * count, width, width), of_g),
            scratch_shapes=[
                pltpu.VMEM((count, len(cores), 2, depth, width), BF16),
                pltpu.VMEM((slots, len(each), depth, width), BF16),
                pltpu.VMEM((len(each), width, depth), BF16),
                pltpu.SemaphoreType.DMA((count, len(cores), max(len(pair[0]) for pair in lefts), 2)),
                pltpu.SemaphoreType.DMA((slots, len(each), parts)),
            ],
        ),
        input_output_aliases={count + len(operands): 0} if extra else {},
        compiler_params=pltpu.CompilerParams(
            dimension_semantics=("arbitrary",), vmem_limit_bytes=VMEM
        ),
        cost_estimate=BRIEF if first == 3 or z_first else LONG,
        name=f"combine_{first}_{z_first}_{cores[0]}",
    )(where, *codes, *operands)


def assemble(where, pieces):
    width = pieces[0][1].shape[-1]
    counts = [piece.shape[0] // 8 for _, piece in pieces]

    def kernel(where, *refs):
        *piece_refs, out_ref = refs
        for (first, _), count, ref in zip(pieces, counts, piece_refs):
            for k in range(count):
                out_ref[0, where[4 + first + k]] = ref[0, :, k]

    at_z = lambda z_j, where: (z_j, 0, 0, 0, 0)
    return pl.pallas_call(
        kernel,
        out_shape=jax.ShapeDtypeStruct((4, 4, 2, width, width), BF16),
        grid_spec=pltpu.PrefetchScalarGridSpec(
            num_scalar_prefetch=1,
            grid=(4,),
            in_specs=[pl.BlockSpec((1, 2, count, width, width), at_z) for count in counts],
            out_specs=pl.BlockSpec((1, 4, 2, width, width), at_z),
        ),
        compiler_params=pltpu.CompilerParams(vmem_limit_bytes=VMEM),
        cost_estimate=BRIEF,
        name="assemble",
    )(where, *[p.reshape(4, 2, n, width, width) for (_, p), n in zip(pieces, counts)])


def pack(wavefunction, pair_left, pair_right):
    width = wavefunction.shape[-1]
    blocks = wavefunction.reshape(4, 4, 2, width, width)

    def kernel(left, right, in_ref, out_ref, buf, in_sems, out_sems):
        copies = []
        for n in range(8):
            copies.append(
                pltpu.make_async_copy(
                    in_ref.at[n // 2, :, n % 2], buf.at[n, :, pl.ds(0, width)], in_sems.at[n]
                )
            )
            copies[n].start()
        lane = lax.broadcasted_iota(jnp.int32, (TAIL, width), 1)
        for n in range(8):
            for x_r in range(4):
                slot = (n // 2 * 4 + x_r) * 2 + n % 2
                picks = jnp.where(lane == 0, left[slot], jnp.where(lane == 1, right[slot], 0))
                buf[n, x_r, width:] = picks.astype(jnp.float32).astype(BF16)
        for n in range(8):
            copies[n].wait()
            copies[n] = pltpu.make_async_copy(buf.at[n], out_ref.at[n], out_sems.at[n])
            copies[n].start()
        for copy in copies:
            copy.wait()

    shape = (8, 4, width + TAIL, width)
    return pl.pallas_call(
        kernel,
        out_shape=jax.ShapeDtypeStruct(shape, BF16),
        grid_spec=pltpu.PrefetchScalarGridSpec(
            num_scalar_prefetch=2,
            grid=(1,),
            in_specs=[pl.BlockSpec(memory_space=pl.ANY)],
            out_specs=pl.BlockSpec(memory_space=pl.ANY),
            scratch_shapes=[
                pltpu.VMEM(shape, BF16),
                pltpu.SemaphoreType.DMA((8,)),
                pltpu.SemaphoreType.DMA((8,)),
            ],
        ),
        compiler_params=pltpu.CompilerParams(vmem_limit_bytes=VMEM),
        cost_estimate=BRIEF,
        name="pack",
    )(pair_left, pair_right, blocks)


def column(psi, position):
    zero = jnp.uint32(0)
    start = (zero, position.astype(jnp.uint32), zero, zero)
    return lax.dynamic_slice(psi, start, (8, 1) + psi.shape[2:])


def split(piece):
    return piece, piece[:, :, -TAIL, :2].astype(jnp.int32).reshape(-1)


def together(*arrays):
    return lax.optimization_barrier(arrays)


def body(where, wavefunction, pair_left, pair_right, left_env, left_dims, right_env, right_dims):
    width = wavefunction.shape[-1]
    sectors, terms = left_env.shape[:2]
    where = where.reshape(-1)

    index = lax.broadcasted_iota(jnp.int32, right_env.shape, 2)
    right_own = jnp.where(index < right_dims[:, None, None, None], right_env, jnp.zeros_like(right_env))
    index = lax.broadcasted_iota(jnp.int32, left_env.shape, 3)
    left_own = jnp.where(index < left_dims[:, None, None, None], left_env, jnp.zeros_like(left_env))
    left_own = left_own.reshape(sectors, terms * width, width)
    right_own = right_own.reshape(sectors, terms * width, width)

    psi = exchange(pack(wavefunction, pair_left, pair_right), ("y", "c"))
    right_low, right_high = both_ways(right_own, "z")
    left_low, left_high = both_ways(left_own, "x")
    left_other = shift(left_own, "c", 1, 2)
    psi, right_low, right_high, left_low, left_high, left_other = together(
        psi, right_low, right_high, left_low, left_high, left_other
    )

    for_low, for_high = column(psi, where[10]), column(psi, where[11])
    for_low, for_high, psi, *to_far = together(for_low, for_high, psi, right_low, right_high)
    psi_low, psi_high = shift(for_low, "x", 1), shift(for_high, "x", 3)
    far = onward(*to_far, "z")
    psi_own = split(psi)
    rights = [(right_own,), (right_low,), (right_high,)]
    lefts_own = [((left_own,), (left_other,))]
    own = combine(where, [psi_own], lefts_own, rights, 0)
    own, psi, left_low, left_high = together(own, psi, left_low, left_high)
    halves = left_low[:, : terms * width // 2], left_high[:, terms * width // 2 :]
    rights.append(tuple(far))
    own = combine(where, [psi_own], lefts_own, rights[3:], 0, 3, own)
    psi_rest, psi_low, psi_high, own, left_low, left_high, *halves = together(
        column(psi, where[12]), psi_low, psi_high, own, left_low, left_high, *halves
    )

    left_far = shift(halves[0], "x", 1), shift(halves[1], "x", 3)
    psi_far = shift(psi_rest, "x", 2)
    own = exchange(own, "z")
    others = [shift(a, "c", 1, 2) for a in (left_low, left_high)]
    psi_low, psi_high, *others = together(psi_low, psi_high, *others)
    lefts_near = [((left_low,), (others[0],)), ((left_high,), (others[1],))]
    near = combine(where, [split(psi_low), split(psi_high)], lefts_near, rights, 1)
    psi_far, *left_far = together(psi_far, *left_far, near)[:-1]
    near = exchange(near, "z")
    other_far = [shift(a, "c", 1, 2) for a in left_far]
    psi_far = split(psi_far)
    rest = combine(where, [psi_far], [(tuple(left_far),)], rights, 3, cores=(0,))
    rest = combine(where, [psi_far], [(tuple(other_far),)], rights, 3, kept=rest, cores=(1,))
    rest = exchange(rest, "z")
    applied = assemble(where, [(0, own), (1, near)])
    zero = jnp.uint32(0)
    applied = lax.dynamic_update_slice(
        applied,
        rest.reshape(4, 1, 2, width, width),
        (zero, where[7].astype(jnp.uint32), zero, zero, zero),
    )
    return applied.reshape(wavefunction.shape)


def solution(mesh):
    fine = Mesh(mesh.devices.reshape(4, 4, 4, 2), AXES)
    mapped = jax.shard_map(
        body, mesh=fine, in_specs=P(AXES), out_specs=P(AXES), check_vma=False
    )

    def run(*arrays):
        return mapped(jnp.asarray(ring_positions()), *arrays)

    return run
```

```python
import jax
import jax.numpy as jnp
import numpy as np
from jax import lax
from jax.experimental import pallas as pl
from jax.experimental.pallas import tpu as pltpu
from jax.sharding import Mesh, PartitionSpec as P

AXES = ("y", "z", "x", "c")
OFFSETS = (0, 3, 1, 2)
STEPS = (0, 1, 3, 2)
TAIL = 16
BF16 = jnp.bfloat16
BRIEF = pl.CostEstimate(flops=1, bytes_accessed=1, transcendentals=0)
LONG = pl.CostEstimate(flops=10**12, bytes_accessed=1, transcendentals=0)
VMEM = 60 * 2**20


def ring_positions():
    rows = []
    for y, z, x, c in np.ndindex(4, 4, 4, 2):
        rows.append(
            [(z + o) % 4 for o in OFFSETS]
            + [(x + o) % 4 for o in OFFSETS]
            + [c]
            + [(x + o) % 4 for o in STEPS]
        )
    return np.asarray(rows, np.int32)


def exchange(array, axis):
    return lax.all_to_all(array, axis, split_axis=0, concat_axis=0, tiled=True)


def shift(array, axis, step, size=4):
    return lax.ppermute(array, axis, [(i, (i + step) % size) for i in range(size)])


def both_ways(array, axis):
    return shift(array, axis, 1), shift(array, axis, 3)


def halves_of(from_low, from_high):
    half = from_low.shape[1] // 2
    return from_low[:, :half], from_high[:, half:]


def onward(halves, axis):
    return shift(halves[0], axis, 1), shift(halves[1], axis, 3)


def combine(where, psis, lefts, rights, first, z_first=0, kept=None, cores=(0, 1)):
    codes = [codes for _, codes in psis]
    psis = [psi for psi, _ in psis]
    width = psis[0].shape[-1]
    columns = psis[0].shape[1]
    depth = sum(a.shape[1] for a in lefts[0][0])
    terms = depth // width
    count = len(lefts)
    left_parts = [a for pair in lefts for group in pair for a in group]
    right_parts = [a for group in rights for a in group]
    steps = len(rights)
    last = steps - 1
    size_out = len(cores) * count
    each = [(core, k) for core in cores for k in range(count)]

    def mine(where):
        return where[9] if columns > 1 else 0

    def pick_of(step, core, k, side, where, codes):
        block = where[z_first + step] * 2 + (where[8] ^ core)
        return codes[k][(block * columns + mine(where)) * 2 + side]

    def kernel(where, *refs):
        codes, refs = refs[:count], list(refs[count:])
        psi_refs = [refs.pop(0) for _ in psis]
        left_refs = [[[refs.pop(0) for _ in group] for group in pair] for pair in lefts]
        right_refs = [[refs.pop(0) for _ in group] for group in rights]
        (out_ref, psi_buf, left_buf, right_buf, partial, out_buf, psi_sems, left_sems, sems, out_sems) = refs[
            kept is not None :
        ]
        step = pl.program_id(0)

        def copy_lefts(needed, go):
            for core, k in each:
                at = core - cores[0]
                pick = pick_of(0, core, k, 0, where, codes)
                pick = pick if needed else 1 - pick
                row = 0
                for n, ref in enumerate(left_refs[k][at]):
                    size = ref.shape[1]
                    copy = pltpu.make_async_copy(
                        ref.at[pick],
                        left_buf.at[k, at, pick, pl.ds(row, size)],
                        left_sems.at[k, at, n, 0 if needed else 1],
                    )
                    copy.start() if go else copy.wait()
                    row += size

        def fetch(n_step, go):
            g = where[z_first + n_step]
            for k in range(count):
                copy = pltpu.make_async_copy(
                    psi_refs[k].at[pl.ds(g * 2, 2), mine(where), pl.ds(0, width)],
                    psi_buf.at[n_step, k],
                    psi_sems.at[n_step, k],
                )
                copy.start() if go else copy.wait()
            for n_block, (core, k) in enumerate(each):
                right = pick_of(n_step, core, k, 1, where, codes)
                row = 0
                for n, ref in enumerate(right_refs[n_step]):
                    size = ref.shape[1]
                    copy = pltpu.make_async_copy(
                        ref.at[right],
                        right_buf.at[n_step, n_block, pl.ds(row, size)],
                        sems.at[n_step, n_block, n],
                    )
                    copy.start() if go else copy.wait()
                    row += size

        def leave(n_step):
            g = where[z_first + n_step]
            to = g * size_out if len(cores) > 1 else (g * 2 + (where[8] ^ cores[0])) * count
            return pltpu.make_async_copy(
                out_buf.at[n_step], out_ref.at[pl.ds(to, size_out)], out_sems.at[n_step]
            )

        @pl.when(step == 0)
        def _():
            copy_lefts(True, True)
            fetch(0, True)
            if steps > 1:
                copy_lefts(False, True)
            for n_step in range(1, steps):
                fetch(n_step, True)
            copy_lefts(True, False)

        if steps > 1:

            @pl.when(step == 1)
            def _():
                copy_lefts(False, False)

        for n_step in range(steps):

            @pl.when(step == n_step)
            def _(n_step=n_step):
                fetch(n_step, False)

        for n_block, (core, k) in enumerate(each):
            left = pick_of(step, core, k, 0, where, codes)
            block = psi_buf[step, k, where[8] ^ core]
            for t in range(terms):
                product = jnp.dot(
                    left_buf[k, core - cores[0], left, t * width : (t + 1) * width],
                    block,
                    preferred_element_type=jnp.float32,
                )
                partial[n_block, :, t * width : (t + 1) * width] = product.astype(BF16)
        for n_block, (core, k) in enumerate(each):
            total = jnp.dot(
                partial[n_block], right_buf[step, n_block], preferred_element_type=jnp.float32
            )
            row = (where[8] ^ core) * count if len(cores) > 1 else 0
            out_buf[step, row + k] = total.astype(BF16)
        for n_step in range(steps):

            @pl.when(step == n_step)
            def _(n_step=n_step):
                leave(n_step).start()

        @pl.when(step == last)
        def _():
            for n_step in range(steps):
                leave(n_step).wait()

    in_place = pl.BlockSpec(memory_space=pl.ANY)
    parts = max(len(group) for group in rights)
    extra = [] if kept is None else [kept]
    operands = [*psis, *left_parts, *right_parts, *extra]
    return pl.pallas_call(
        kernel,
        out_shape=jax.ShapeDtypeStruct((8 * count, width, width), BF16),
        grid_spec=pltpu.PrefetchScalarGridSpec(
            num_scalar_prefetch=1 + count,
            grid=(steps,),
            in_specs=[in_place] * len(operands),
            out_specs=in_place,
            scratch_shapes=[
                pltpu.VMEM((steps, count, 2, width, width), BF16),
                pltpu.VMEM((count, len(cores), 2, depth, width), BF16),
                pltpu.VMEM((steps, len(each), depth, width), BF16),
                pltpu.VMEM((len(each), width, depth), BF16),
                pltpu.VMEM((steps, size_out, width, width), BF16),
                pltpu.SemaphoreType.DMA((steps, count)),
                pltpu.SemaphoreType.DMA((count, len(cores), max(len(pair[0]) for pair in lefts), 2)),
                pltpu.SemaphoreType.DMA((steps, len(each), parts)),
                pltpu.SemaphoreType.DMA((steps,)),
            ],
        ),
        input_output_aliases={count + len(operands): 0} if extra else {},
        compiler_params=pltpu.CompilerParams(
            dimension_semantics=("arbitrary",), vmem_limit_bytes=VMEM
        ),
        cost_estimate=BRIEF if first == 3 or z_first else LONG,
        name=f"combine_{first}_{z_first}_{cores[0]}",
    )(where, *codes, *operands)


def assemble(where, pieces):
    width = pieces[0][1].shape[-1]
    counts = [piece.shape[0] // 8 for _, piece in pieces]

    def kernel(where, *refs):
        *piece_refs, out_ref = refs
        for (first, _), count, ref in zip(pieces, counts, piece_refs):
            for k in range(count):
                out_ref[0, where[4 + first + k]] = ref[0, :, k]

    at_z = lambda z_j, where: (z_j, 0, 0, 0, 0)
    return pl.pallas_call(
        kernel,
        out_shape=jax.ShapeDtypeStruct((4, 4, 2, width, width), BF16),
        grid_spec=pltpu.PrefetchScalarGridSpec(
            num_scalar_prefetch=1,
            grid=(4,),
            in_specs=[pl.BlockSpec((1, 2, count, width, width), at_z) for count in counts],
            out_specs=pl.BlockSpec((1, 4, 2, width, width), at_z),
        ),
        compiler_params=pltpu.CompilerParams(vmem_limit_bytes=VMEM),
        cost_estimate=BRIEF,
        name="assemble",
    )(where, *[p.reshape(4, 2, n, width, width) for (_, p), n in zip(pieces, counts)])


def pack(wavefunction, pair_left, pair_right):
    width = wavefunction.shape[-1]
    blocks = wavefunction.reshape(4, 4, 2, width, width)

    def kernel(left, right, in_ref, out_ref, buf, in_sems, out_sems):
        copies = []
        for n in range(8):
            copies.append(
                pltpu.make_async_copy(
                    in_ref.at[n // 2, :, n % 2], buf.at[n, :, pl.ds(0, width)], in_sems.at[n]
                )
            )
            copies[n].start()
        lane = lax.broadcasted_iota(jnp.int32, (TAIL, width), 1)
        for n in range(8):
            for x_r in range(4):
                slot = (n // 2 * 4 + x_r) * 2 + n % 2
                picks = jnp.where(lane == 0, left[slot], jnp.where(lane == 1, right[slot], 0))
                buf[n, x_r, width:] = picks.astype(jnp.float32).astype(BF16)
        for n in range(8):
            copies[n].wait()
            copies[n] = pltpu.make_async_copy(buf.at[n], out_ref.at[n], out_sems.at[n])
            copies[n].start()
        for copy in copies:
            copy.wait()

    shape = (8, 4, width + TAIL, width)
    return pl.pallas_call(
        kernel,
        out_shape=jax.ShapeDtypeStruct(shape, BF16),
        grid_spec=pltpu.PrefetchScalarGridSpec(
            num_scalar_prefetch=2,
            grid=(1,),
            in_specs=[pl.BlockSpec(memory_space=pl.ANY)],
            out_specs=pl.BlockSpec(memory_space=pl.ANY),
            scratch_shapes=[
                pltpu.VMEM(shape, BF16),
                pltpu.SemaphoreType.DMA((8,)),
                pltpu.SemaphoreType.DMA((8,)),
            ],
        ),
        compiler_params=pltpu.CompilerParams(vmem_limit_bytes=VMEM),
        cost_estimate=BRIEF,
        name="pack",
    )(pair_left, pair_right, blocks)


def column(psi, position):
    zero = jnp.uint32(0)
    start = (zero, position.astype(jnp.uint32), zero, zero)
    return lax.dynamic_slice(psi, start, (8, 1) + psi.shape[2:])


def split(piece):
    return piece, piece[:, :, -TAIL, :2].astype(jnp.int32).reshape(-1)


def together(*arrays):
    return lax.optimization_barrier(arrays)


def body(where, wavefunction, pair_left, pair_right, left_env, left_dims, right_env, right_dims):
    width = wavefunction.shape[-1]
    sectors, terms = left_env.shape[:2]
    where = where.reshape(-1)

    index = lax.broadcasted_iota(jnp.int32, right_env.shape, 2)
    right_own = jnp.where(index < right_dims[:, None, None, None], right_env, jnp.zeros_like(right_env))
    index = lax.broadcasted_iota(jnp.int32, left_env.shape, 3)
    left_own = jnp.where(index < left_dims[:, None, None, None], left_env, jnp.zeros_like(left_env))
    left_own = left_own.reshape(sectors, terms * width, width)
    right_own = right_own.reshape(sectors, terms * width, width)

    psi = exchange(pack(wavefunction, pair_left, pair_right), ("y", "c"))
    right_low, right_high = both_ways(right_own, "z")
    left_low, left_high = both_ways(left_own, "x")
    left_other = shift(left_own, "c", 1, 2)
    psi, right_low, right_high, left_low, left_high, left_other, *to_far = together(
        psi, right_low, right_high, left_low, left_high, left_other, *halves_of(right_low, right_high)
    )

    for_low, for_high = column(psi, where[10]), column(psi, where[11])
    for_low, for_high, psi, *to_far = together(for_low, for_high, psi, *to_far)
    psi_low, psi_high = shift(for_low, "x", 1), shift(for_high, "x", 3)
    far = onward(to_far, "z")
    psi_own = split(psi)
    rights = [(right_own,), (right_low,), (right_high,)]
    lefts_own = [((left_own,), (left_other,))]
    own = combine(where, [psi_own], lefts_own, rights, 0)
    own, psi, left_low, left_high = together(own, psi, left_low, left_high)
    halves = halves_of(left_low, left_high)
    rights.append(tuple(far))
    own = combine(where, [psi_own], lefts_own, rights[3:], 0, 3, own)
    psi_rest, psi_low, psi_high, own, left_low, left_high, *halves = together(
        column(psi, where[12]), psi_low, psi_high, own, left_low, left_high, *halves
    )

    left_far = onward(halves, "x")
    psi_far = shift(psi_rest, "x", 2)
    own = exchange(own, "z")
    others = [shift(a, "c", 1, 2) for a in (left_low, left_high)]
    psi_low, psi_high, *others = together(psi_low, psi_high, *others)
    lefts_near = [((left_low,), (others[0],)), ((left_high,), (others[1],))]
    near = combine(where, [split(psi_low), split(psi_high)], lefts_near, rights, 1)
    psi_far, *left_far = together(psi_far, *left_far, near)[:-1]
    near = exchange(near, "z")
    other_far = [shift(a, "c", 1, 2) for a in left_far]
    psi_far = split(psi_far)
    rest = combine(where, [psi_far], [(tuple(left_far), tuple(other_far))], rights, 3)
    rest = exchange(rest, "z")
    applied = assemble(where, [(0, own), (1, near)])
    zero = jnp.uint32(0)
    applied = lax.dynamic_update_slice(
        applied,
        rest.reshape(4, 1, 2, width, width),
        (zero, where[7].astype(jnp.uint32), zero, zero, zero),
    )
    return applied.reshape(wavefunction.shape)


def solution(mesh):
    fine = Mesh(mesh.devices.reshape(4, 4, 4, 2), AXES)
    mapped = jax.shard_map(
        body, mesh=fine, in_specs=P(AXES), out_specs=P(AXES), check_vma=False
    )

    def run(*arrays):
        return mapped(jnp.asarray(ring_positions()), *arrays)

    return run
```

```python
import jax
import jax.numpy as jnp
import numpy as np
from jax import lax
from jax.experimental import pallas as pl
from jax.experimental.pallas import tpu as pltpu
from jax.sharding import Mesh, PartitionSpec as P

AXES = ("y", "z", "x", "c")
OFFSETS = (0, 3, 1, 2)
STEPS = (0, 1, 3, 2)
TAIL = 16
BF16 = jnp.bfloat16
BRIEF = pl.CostEstimate(flops=1, bytes_accessed=1, transcendentals=0)
LONG = pl.CostEstimate(flops=10**12, bytes_accessed=1, transcendentals=0)
VMEM = 60 * 2**20


def ring_positions():
    rows = []
    for y, z, x, c in np.ndindex(4, 4, 4, 2):
        rows.append(
            [(z + o) % 4 for o in OFFSETS]
            + [(x + o) % 4 for o in OFFSETS]
            + [c]
            + [(x + o) % 4 for o in STEPS]
        )
    return np.asarray(rows, np.int32)


def exchange(array, axis):
    return lax.all_to_all(array, axis, split_axis=0, concat_axis=0, tiled=True)


def shift(array, axis, step, size=4):
    return lax.ppermute(array, axis, [(i, (i + step) % size) for i in range(size)])


def both_ways(array, axis):
    return shift(array, axis, 1), shift(array, axis, 3)


def halves_of(from_low, from_high):
    half = from_low.shape[1] // 2
    return from_low[:, :half], from_high[:, half:]


def onward(halves, axis):
    return shift(halves[0], axis, 1), shift(halves[1], axis, 3)


def when(condition):
    if isinstance(condition, bool):
        return (lambda then: then()) if condition else (lambda then: None)
    return pl.when(condition)


def combine(where, psis, lefts, rights, first, z_first=0, kept=None, cores=(0, 1)):
    codes = [codes for _, codes in psis]
    psis = [psi for psi, _ in psis]
    width = psis[0].shape[-1]
    columns = psis[0].shape[1]
    depth = sum(a.shape[1] for a in lefts[0][0])
    terms = depth // width
    count = len(lefts)
    left_parts = [a for pair in lefts for group in pair for a in group]
    right_parts = [a for group in rights for a in group]
    steps = len(rights)
    last = steps - 1
    unrolled = count == 1
    size_out = len(cores) * count
    each = [(core, k) for core in cores for k in range(count)]

    def mine(where):
        return where[9] if columns > 1 else 0

    def pick_of(step, core, k, side, where, codes):
        block = where[z_first + step] * 2 + (where[8] ^ core)
        return codes[k][(block * columns + mine(where)) * 2 + side]

    def kernel(where, *refs):
        codes, refs = refs[:count], list(refs[count:])
        psi_refs = [refs.pop(0) for _ in psis]
        left_refs = [[[refs.pop(0) for _ in group] for group in pair] for pair in lefts]
        right_refs = [[refs.pop(0) for _ in group] for group in rights]
        (out_ref, psi_buf, left_buf, right_buf, partial, out_buf, psi_sems, left_sems, sems, out_sems) = refs[
            kept is not None :
        ]
        def copy_lefts(needed, go):
            for core, k in each:
                at = core - cores[0]
                pick = pick_of(0, core, k, 0, where, codes)
                pick = pick if needed else 1 - pick
                row = 0
                for n, ref in enumerate(left_refs[k][at]):
                    size = ref.shape[1]
                    copy = pltpu.make_async_copy(
                        ref.at[pick],
                        left_buf.at[k, at, pick, pl.ds(row, size)],
                        left_sems.at[k, at, n, 0 if needed else 1],
                    )
                    copy.start() if go else copy.wait()
                    row += size

        def fetch(n_step, go):
            g = where[z_first + n_step]
            for k in range(count):
                copy = pltpu.make_async_copy(
                    psi_refs[k].at[pl.ds(g * 2, 2), mine(where), pl.ds(0, width)],
                    psi_buf.at[n_step, k],
                    psi_sems.at[n_step, k],
                )
                copy.start() if go else copy.wait()
            for n_block, (core, k) in enumerate(each):
                right = pick_of(n_step, core, k, 1, where, codes)
                row = 0
                for n, ref in enumerate(right_refs[n_step]):
                    size = ref.shape[1]
                    copy = pltpu.make_async_copy(
                        ref.at[right],
                        right_buf.at[n_step, n_block, pl.ds(row, size)],
                        sems.at[n_step, n_block, n],
                    )
                    copy.start() if go else copy.wait()
                    row += size

        def leave(n_step):
            g = where[z_first + n_step]
            to = g * size_out if len(cores) > 1 else (g * 2 + (where[8] ^ cores[0])) * count
            return pltpu.make_async_copy(
                out_buf.at[n_step], out_ref.at[pl.ds(to, size_out)], out_sems.at[n_step]
            )

        def run(step):
            @when(step == 0)
            def _():
                copy_lefts(True, True)
                fetch(0, True)
                if steps > 1:
                    copy_lefts(False, True)
                for n_step in range(1, steps):
                    fetch(n_step, True)
                copy_lefts(True, False)

            if steps > 1:

                @when(step == 1)
                def _():
                    copy_lefts(False, False)

            for n_step in range(steps):

                @when(step == n_step)
                def _(n_step=n_step):
                    fetch(n_step, False)

            for n_block, (core, k) in enumerate(each):
                left = pick_of(step, core, k, 0, where, codes)
                block = psi_buf[step, k, where[8] ^ core]
                for t in range(terms):
                    product = jnp.dot(
                        left_buf[k, core - cores[0], left, t * width : (t + 1) * width],
                        block,
                        preferred_element_type=jnp.float32,
                    )
                    partial[n_block, :, t * width : (t + 1) * width] = product.astype(BF16)
            for n_block, (core, k) in enumerate(each):
                total = jnp.dot(
                    partial[n_block], right_buf[step, n_block], preferred_element_type=jnp.float32
                )
                row = (where[8] ^ core) * count if len(cores) > 1 else 0
                out_buf[step, row + k] = total.astype(BF16)
            for n_step in range(steps):

                @when(step == n_step)
                def _(n_step=n_step):
                    leave(n_step).start()

            @when(step == last)
            def _():
                for n_step in range(steps):
                    leave(n_step).wait()

        for step in range(steps) if unrolled else [pl.program_id(0)]:
            run(step)

    in_place = pl.BlockSpec(memory_space=pl.ANY)
    parts = max(len(group) for group in rights)
    extra = [] if kept is None else [kept]
    operands = [*psis, *left_parts, *right_parts, *extra]
    return pl.pallas_call(
        kernel,
        out_shape=jax.ShapeDtypeStruct((8 * count, width, width), BF16),
        grid_spec=pltpu.PrefetchScalarGridSpec(
            num_scalar_prefetch=1 + count,
            grid=(1 if unrolled else steps,),
            in_specs=[in_place] * len(operands),
            out_specs=in_place,
            scratch_shapes=[
                pltpu.VMEM((steps, count, 2, width, width), BF16),
                pltpu.VMEM((count, len(cores), 2, depth, width), BF16),
                pltpu.VMEM((steps, len(each), depth, width), BF16),
                pltpu.VMEM((len(each), width, depth), BF16),
                pltpu.VMEM((steps, size_out, width, width), BF16),
                pltpu.SemaphoreType.DMA((steps, count)),
                pltpu.SemaphoreType.DMA((count, len(cores), max(len(pair[0]) for pair in lefts), 2)),
                pltpu.SemaphoreType.DMA((steps, len(each), parts)),
                pltpu.SemaphoreType.DMA((steps,)),
            ],
        ),
        input_output_aliases={count + len(operands): 0} if extra else {},
        compiler_params=pltpu.CompilerParams(
            dimension_semantics=("arbitrary",), vmem_limit_bytes=VMEM
        ),
        cost_estimate=BRIEF if first == 3 or z_first else LONG,
        name=f"combine_{first}_{z_first}_{cores[0]}",
    )(where, *codes, *operands)


def assemble(where, pieces):
    width = pieces[0][1].shape[-1]
    counts = [piece.shape[0] // 8 for _, piece in pieces]

    def kernel(where, *refs):
        *piece_refs, out_ref = refs
        for (first, _), count, ref in zip(pieces, counts, piece_refs):
            for k in range(count):
                out_ref[0, where[4 + first + k]] = ref[0, :, k]

    at_z = lambda z_j, where: (z_j, 0, 0, 0, 0)
    return pl.pallas_call(
        kernel,
        out_shape=jax.ShapeDtypeStruct((4, 4, 2, width, width), BF16),
        grid_spec=pltpu.PrefetchScalarGridSpec(
            num_scalar_prefetch=1,
            grid=(4,),
            in_specs=[pl.BlockSpec((1, 2, count, width, width), at_z) for count in counts],
            out_specs=pl.BlockSpec((1, 4, 2, width, width), at_z),
        ),
        compiler_params=pltpu.CompilerParams(vmem_limit_bytes=VMEM),
        cost_estimate=BRIEF,
        name="assemble",
    )(where, *[p.reshape(4, 2, n, width, width) for (_, p), n in zip(pieces, counts)])


def pack(wavefunction, pair_left, pair_right):
    width = wavefunction.shape[-1]
    blocks = wavefunction.reshape(4, 4, 2, width, width)

    def kernel(left, right, in_ref, out_ref, buf, in_sems, out_sems):
        copies = []
        for n in range(8):
            copies.append(
                pltpu.make_async_copy(
                    in_ref.at[n // 2, :, n % 2], buf.at[n, :, pl.ds(0, width)], in_sems.at[n]
                )
            )
            copies[n].start()
        lane = lax.broadcasted_iota(jnp.int32, (TAIL, width), 1)
        for n in range(8):
            for x_r in range(4):
                slot = (n // 2 * 4 + x_r) * 2 + n % 2
                picks = jnp.where(lane == 0, left[slot], jnp.where(lane == 1, right[slot], 0))
                buf[n, x_r, width:] = picks.astype(jnp.float32).astype(BF16)
        for n in range(8):
            copies[n].wait()
            copies[n] = pltpu.make_async_copy(buf.at[n], out_ref.at[n], out_sems.at[n])
            copies[n].start()
        for copy in copies:
            copy.wait()

    shape = (8, 4, width + TAIL, width)
    return pl.pallas_call(
        kernel,
        out_shape=jax.ShapeDtypeStruct(shape, BF16),
        grid_spec=pltpu.PrefetchScalarGridSpec(
            num_scalar_prefetch=2,
            grid=(1,),
            in_specs=[pl.BlockSpec(memory_space=pl.ANY)],
            out_specs=pl.BlockSpec(memory_space=pl.ANY),
            scratch_shapes=[
                pltpu.VMEM(shape, BF16),
                pltpu.SemaphoreType.DMA((8,)),
                pltpu.SemaphoreType.DMA((8,)),
            ],
        ),
        compiler_params=pltpu.CompilerParams(vmem_limit_bytes=VMEM),
        cost_estimate=BRIEF,
        name="pack",
    )(pair_left, pair_right, blocks)


def column(psi, position):
    zero = jnp.uint32(0)
    start = (zero, position.astype(jnp.uint32), zero, zero)
    return lax.dynamic_slice(psi, start, (8, 1) + psi.shape[2:])


def split(piece):
    return piece, piece[:, :, -TAIL, :2].astype(jnp.int32).reshape(-1)


def together(*arrays):
    return lax.optimization_barrier(arrays)


def body(where, wavefunction, pair_left, pair_right, left_env, left_dims, right_env, right_dims):
    width = wavefunction.shape[-1]
    sectors, terms = left_env.shape[:2]
    where = where.reshape(-1)

    index = lax.broadcasted_iota(jnp.int32, right_env.shape, 2)
    right_own = jnp.where(index < right_dims[:, None, None, None], right_env, jnp.zeros_like(right_env))
    index = lax.broadcasted_iota(jnp.int32, left_env.shape, 3)
    left_own = jnp.where(index < left_dims[:, None, None, None], left_env, jnp.zeros_like(left_env))
    left_own = left_own.reshape(sectors, terms * width, width)
    right_own = right_own.reshape(sectors, terms * width, width)

    psi = exchange(pack(wavefunction, pair_left, pair_right), ("y", "c"))
    right_low, right_high = both_ways(right_own, "z")
    left_low, left_high = both_ways(left_own, "x")
    left_other = shift(left_own, "c", 1, 2)
    psi, right_low, right_high, left_low, left_high, left_other, *to_far = together(
        psi, right_low, right_high, left_low, left_high, left_other, *halves_of(right_low, right_high)
    )

    for_low, for_high = column(psi, where[10]), column(psi, where[11])
    for_low, for_high, psi, *to_far = together(for_low, for_high, psi, *to_far)
    psi_low, psi_high = shift(for_low, "x", 1), shift(for_high, "x", 3)
    far = onward(to_far, "z")
    psi_own = split(psi)
    rights = [(right_own,), (right_low,), (right_high,)]
    lefts_own = [((left_own,), (left_other,))]
    own = combine(where, [psi_own], lefts_own, rights, 0)
    own, psi, left_low, left_high = together(own, psi, left_low, left_high)
    halves = halves_of(left_low, left_high)
    rights.append(tuple(far))
    own = combine(where, [psi_own], lefts_own, rights[3:], 0, 3, own)
    psi_rest, psi_low, psi_high, own, left_low, left_high, *halves = together(
        column(psi, where[12]), psi_low, psi_high, own, left_low, left_high, *halves
    )

    left_far = onward(halves, "x")
    psi_far = shift(psi_rest, "x", 2)
    own = exchange(own, "z")
    others = [shift(a, "c", 1, 2) for a in (left_low, left_high)]
    psi_low, psi_high, *others = together(psi_low, psi_high, *others)
    lefts_near = [((left_low,), (others[0],)), ((left_high,), (others[1],))]
    near = combine(where, [split(psi_low), split(psi_high)], lefts_near, rights, 1)
    psi_far, *left_far = together(psi_far, *left_far, near)[:-1]
    near = exchange(near, "z")
    other_far = [shift(a, "c", 1, 2) for a in left_far]
    psi_far = split(psi_far)
    rest = combine(where, [psi_far], [(tuple(left_far), tuple(other_far))], rights, 3)
    rest = exchange(rest, "z")
    applied = assemble(where, [(0, own), (1, near)])
    zero = jnp.uint32(0)
    applied = lax.dynamic_update_slice(
        applied,
        rest.reshape(4, 1, 2, width, width),
        (zero, where[7].astype(jnp.uint32), zero, zero, zero),
    )
    return applied.reshape(wavefunction.shape)


def solution(mesh):
    fine = Mesh(mesh.devices.reshape(4, 4, 4, 2), AXES)
    mapped = jax.shard_map(
        body, mesh=fine, in_specs=P(AXES), out_specs=P(AXES), check_vma=False
    )

    def run(*arrays):
        return mapped(jnp.asarray(ring_positions()), *arrays)

    return run
```

```python
import jax
import jax.numpy as jnp
import numpy as np
from jax import lax
from jax.experimental import pallas as pl
from jax.experimental.pallas import tpu as pltpu
from jax.sharding import Mesh, PartitionSpec as P

AXES = ("y", "z", "x", "c")
OFFSETS = (0, 3, 1, 2)
STEPS = (0, 1, 3, 2)
TAIL = 16
BF16 = jnp.bfloat16
BRIEF = pl.CostEstimate(flops=1, bytes_accessed=1, transcendentals=0)
LONG = pl.CostEstimate(flops=10**12, bytes_accessed=1, transcendentals=0)
VMEM = 62 * 2**20


def ring_positions():
    rows = []
    for y, z, x, c in np.ndindex(4, 4, 4, 2):
        rows.append(
            [(z + o) % 4 for o in OFFSETS]
            + [(x + o) % 4 for o in OFFSETS]
            + [c]
            + [(x + o) % 4 for o in STEPS]
        )
    return np.asarray(rows, np.int32)


def exchange(array, axis):
    return lax.all_to_all(array, axis, split_axis=0, concat_axis=0, tiled=True)


def shift(array, axis, step, size=4):
    return lax.ppermute(array, axis, [(i, (i + step) % size) for i in range(size)])


def both_ways(array, axis):
    return shift(array, axis, 1), shift(array, axis, 3)


def halves_of(from_low, from_high):
    half = from_low.shape[1] // 2
    return from_low[:, :half], from_high[:, half:]


def onward(halves, axis):
    return shift(halves[0], axis, 1), shift(halves[1], axis, 3)


def combine(where, psis, lefts, rights, first, z_first=0, kept=None, cores=(0, 1)):
    codes = [codes for _, codes in psis]
    psis = [psi for psi, _ in psis]
    width = psis[0].shape[-1]
    columns = psis[0].shape[1]
    depth = sum(a.shape[1] for a in lefts[0][0])
    terms = depth // width
    count = len(lefts)
    left_parts = [a for pair in lefts for group in pair for a in group]
    right_parts = [a for group in rights for a in group]
    steps = len(rights)
    last = steps - 1
    size_out = len(cores) * count
    each = [(core, k) for core in cores for k in range(count)]

    def mine(where):
        return where[9] if columns > 1 else 0

    def pick_of(step, core, k, side, where, codes):
        block = where[z_first + step] * 2 + (where[8] ^ core)
        return codes[k][(block * columns + mine(where)) * 2 + side]

    def kernel(where, *refs):
        codes, refs = refs[:count], list(refs[count:])
        psi_refs = [refs.pop(0) for _ in psis]
        left_refs = [[[refs.pop(0) for _ in group] for group in pair] for pair in lefts]
        right_refs = [[refs.pop(0) for _ in group] for group in rights]
        (out_ref, psi_buf, left_buf, right_buf, partial, out_buf, psi_sems, left_sems, sems, out_sems) = refs[
            kept is not None :
        ]
        step = pl.program_id(0)

        def copy_lefts(needed, go):
            for core, k in each:
                at = core - cores[0]
                pick = pick_of(0, core, k, 0, where, codes)
                pick = pick if needed else 1 - pick
                row = 0
                for n, ref in enumerate(left_refs[k][at]):
                    size = ref.shape[1]
                    copy = pltpu.make_async_copy(
                        ref.at[pick],
                        left_buf.at[k, at, pick, pl.ds(row, size)],
                        left_sems.at[k, at, n, 0 if needed else 1],
                    )
                    copy.start() if go else copy.wait()
                    row += size

        def fetch(n_step, go):
            g = where[z_first + n_step]
            for k in range(count):
                copy = pltpu.make_async_copy(
                    psi_refs[k].at[pl.ds(g * 2, 2), mine(where), pl.ds(0, width)],
                    psi_buf.at[n_step, k],
                    psi_sems.at[n_step, k],
                )
                copy.start() if go else copy.wait()
            for n_block, (core, k) in enumerate(each):
                right = pick_of(n_step, core, k, 1, where, codes)
                row = 0
                for n, ref in enumerate(right_refs[n_step]):
                    size = ref.shape[1]
                    copy = pltpu.make_async_copy(
                        ref.at[right],
                        right_buf.at[n_step, n_block, pl.ds(row, size)],
                        sems.at[n_step, n_block, n],
                    )
                    copy.start() if go else copy.wait()
                    row += size

        def leave(n_step):
            g = where[z_first + n_step]
            to = g * size_out if len(cores) > 1 else (g * 2 + (where[8] ^ cores[0])) * count
            return pltpu.make_async_copy(
                out_buf.at[n_step], out_ref.at[pl.ds(to, size_out)], out_sems.at[n_step]
            )

        @pl.when(step == 0)
        def _():
            copy_lefts(True, True)
            fetch(0, True)
            if steps > 1:
                copy_lefts(False, True)
            for n_step in range(1, steps):
                fetch(n_step, True)
            copy_lefts(True, False)

        if steps > 1:

            @pl.when(step == 1)
            def _():
                copy_lefts(False, False)

        for n_step in range(steps):

            @pl.when(step == n_step)
            def _(n_step=n_step):
                fetch(n_step, False)

        for n_block, (core, k) in enumerate(each):
            left = pick_of(step, core, k, 0, where, codes)
            block = psi_buf[step, k, where[8] ^ core]
            for t in range(terms):
                product = jnp.dot(
                    left_buf[k, core - cores[0], left, t * width : (t + 1) * width],
                    block,
                    preferred_element_type=jnp.float32,
                )
                partial[n_block, :, t * width : (t + 1) * width] = product.astype(BF16)
        for n_block, (core, k) in enumerate(each):
            total = jnp.dot(
                partial[n_block], right_buf[step, n_block], preferred_element_type=jnp.float32
            )
            row = (where[8] ^ core) * count if len(cores) > 1 else 0
            out_buf[step, row + k] = total.astype(BF16)
        for n_step in range(steps):

            @pl.when(step == n_step)
            def _(n_step=n_step):
                leave(n_step).start()

        @pl.when(step == last)
        def _():
            for n_step in range(steps):
                leave(n_step).wait()

    in_place = pl.BlockSpec(memory_space=pl.ANY)
    parts = max(len(group) for group in rights)
    extra = [] if kept is None else [kept]
    operands = [*psis, *left_parts, *right_parts, *extra]
    return pl.pallas_call(
        kernel,
        out_shape=jax.ShapeDtypeStruct((8 * count, width, width), BF16),
        grid_spec=pltpu.PrefetchScalarGridSpec(
            num_scalar_prefetch=1 + count,
            grid=(steps,),
            in_specs=[in_place] * len(operands),
            out_specs=in_place,
            scratch_shapes=[
                pltpu.VMEM((steps, count, 2, width, width), BF16),
                pltpu.VMEM((count, len(cores), 2, depth, width), BF16),
                pltpu.VMEM((steps, len(each), depth, width), BF16),
                pltpu.VMEM((len(each), width, depth), BF16),
                pltpu.VMEM((steps, size_out, width, width), BF16),
                pltpu.SemaphoreType.DMA((steps, count)),
                pltpu.SemaphoreType.DMA((count, len(cores), max(len(pair[0]) for pair in lefts), 2)),
                pltpu.SemaphoreType.DMA((steps, len(each), parts)),
                pltpu.SemaphoreType.DMA((steps,)),
            ],
        ),
        input_output_aliases={count + len(operands): 0} if extra else {},
        compiler_params=pltpu.CompilerParams(
            dimension_semantics=("arbitrary",), vmem_limit_bytes=VMEM
        ),
        cost_estimate=BRIEF if first == 3 or z_first else LONG,
        name=f"combine_{first}_{z_first}_{cores[0]}",
    )(where, *codes, *operands)


def assemble(where, pieces):
    width = pieces[0][1].shape[-1]
    counts = [piece.shape[0] // 8 for _, piece in pieces]

    def kernel(where, *refs):
        *piece_refs, out_ref = refs
        for (first, _), count, ref in zip(pieces, counts, piece_refs):
            for k in range(count):
                out_ref[0, where[4 + first + k]] = ref[0, :, k]

    at_z = lambda z_j, where: (z_j, 0, 0, 0, 0)
    return pl.pallas_call(
        kernel,
        out_shape=jax.ShapeDtypeStruct((4, 4, 2, width, width), BF16),
        grid_spec=pltpu.PrefetchScalarGridSpec(
            num_scalar_prefetch=1,
            grid=(4,),
            in_specs=[pl.BlockSpec((1, 2, count, width, width), at_z) for count in counts],
            out_specs=pl.BlockSpec((1, 4, 2, width, width), at_z),
        ),
        compiler_params=pltpu.CompilerParams(vmem_limit_bytes=VMEM),
        cost_estimate=BRIEF,
        name="assemble",
    )(where, *[p.reshape(4, 2, n, width, width) for (_, p), n in zip(pieces, counts)])


def pack(wavefunction, pair_left, pair_right):
    width = wavefunction.shape[-1]
    blocks = wavefunction.reshape(4, 4, 2, width, width)

    def kernel(left, right, in_ref, out_ref, buf, in_sems, out_sems):
        copies = []
        for n in range(8):
            copies.append(
                pltpu.make_async_copy(
                    in_ref.at[n // 2, :, n % 2], buf.at[n, :, pl.ds(0, width)], in_sems.at[n]
                )
            )
            copies[n].start()
        lane = lax.broadcasted_iota(jnp.int32, (TAIL, width), 1)
        for n in range(8):
            for x_r in range(4):
                slot = (n // 2 * 4 + x_r) * 2 + n % 2
                picks = jnp.where(lane == 0, left[slot], jnp.where(lane == 1, right[slot], 0))
                buf[n, x_r, width:] = picks.astype(jnp.float32).astype(BF16)
        for n in range(8):
            copies[n].wait()
            copies[n] = pltpu.make_async_copy(buf.at[n], out_ref.at[n], out_sems.at[n])
            copies[n].start()
        for copy in copies:
            copy.wait()

    shape = (8, 4, width + TAIL, width)
    return pl.pallas_call(
        kernel,
        out_shape=jax.ShapeDtypeStruct(shape, BF16),
        grid_spec=pltpu.PrefetchScalarGridSpec(
            num_scalar_prefetch=2,
            grid=(1,),
            in_specs=[pl.BlockSpec(memory_space=pl.ANY)],
            out_specs=pl.BlockSpec(memory_space=pl.ANY),
            scratch_shapes=[
                pltpu.VMEM(shape, BF16),
                pltpu.SemaphoreType.DMA((8,)),
                pltpu.SemaphoreType.DMA((8,)),
            ],
        ),
        compiler_params=pltpu.CompilerParams(vmem_limit_bytes=VMEM),
        cost_estimate=BRIEF,
        name="pack",
    )(pair_left, pair_right, blocks)


def column(psi, position):
    zero = jnp.uint32(0)
    start = (zero, position.astype(jnp.uint32), zero, zero)
    return lax.dynamic_slice(psi, start, (8, 1) + psi.shape[2:])


def split(piece):
    return piece, piece[:, :, -TAIL, :2].astype(jnp.int32).reshape(-1)


def together(*arrays):
    return lax.optimization_barrier(arrays)


def body(where, wavefunction, pair_left, pair_right, left_env, left_dims, right_env, right_dims):
    width = wavefunction.shape[-1]
    sectors, terms = left_env.shape[:2]
    where = where.reshape(-1)

    index = lax.broadcasted_iota(jnp.int32, right_env.shape, 2)
    right_own = jnp.where(index < right_dims[:, None, None, None], right_env, jnp.zeros_like(right_env))
    index = lax.broadcasted_iota(jnp.int32, left_env.shape, 3)
    left_own = jnp.where(index < left_dims[:, None, None, None], left_env, jnp.zeros_like(left_env))
    left_own = left_own.reshape(sectors, terms * width, width)
    right_own = right_own.reshape(sectors, terms * width, width)

    psi = exchange(pack(wavefunction, pair_left, pair_right), ("y", "c"))
    right_low, right_high = both_ways(right_own, "z")
    left_low, left_high = both_ways(left_own, "x")
    left_other = shift(left_own, "c", 1, 2)
    columns = column(psi, where[10]), column(psi, where[11])
    psi, picks = split(psi)
    psi, picks, for_low, for_high, right_low, right_high = together(psi, picks, *columns, right_low, right_high)
    to_far = halves_of(right_low, right_high)
    left_low, left_high, left_other, for_low, for_high, *to_far = together(
        left_low, left_high, left_other, for_low, for_high, *to_far
    )

    psi_low, psi_high = shift(for_low, "x", 1), shift(for_high, "x", 3)
    far = onward(to_far, "z")
    psi_own = psi, picks
    rights = [(right_own,), (right_low,), (right_high,)]
    lefts_own = [((left_own,), (left_other,))]
    own = combine(where, [psi_own], lefts_own, rights, 0)
    own, psi, left_low, left_high = together(own, psi, left_low, left_high)
    halves = halves_of(left_low, left_high)
    rights.append(tuple(far))
    own = combine(where, [psi_own], lefts_own, rights[3:], 0, 3, own)
    psi_rest, psi_low, psi_high, own, left_low, left_high, *halves = together(
        column(psi, where[12]), psi_low, psi_high, own, left_low, left_high, *halves
    )

    left_far = onward(halves, "x")
    psi_far = shift(psi_rest, "x", 2)
    own = exchange(own, "z")
    others = [shift(a, "c", 1, 2) for a in (left_low, left_high)]
    psi_low, psi_high, *others = together(psi_low, psi_high, *others)
    lefts_near = [((left_low,), (others[0],)), ((left_high,), (others[1],))]
    near = combine(where, [split(psi_low), split(psi_high)], lefts_near, rights, 1)
    psi_far, *left_far = together(psi_far, *left_far, near)[:-1]
    near = exchange(near, "z")
    other_far = [shift(a, "c", 1, 2) for a in left_far]
    psi_far = split(psi_far)
    rest = combine(where, [psi_far], [(tuple(left_far), tuple(other_far))], rights, 3)
    rest = exchange(rest, "z")
    applied = assemble(where, [(0, own), (1, near)])
    zero = jnp.uint32(0)
    applied = lax.dynamic_update_slice(
        applied,
        rest.reshape(4, 1, 2, width, width),
        (zero, where[7].astype(jnp.uint32), zero, zero, zero),
    )
    return applied.reshape(wavefunction.shape)


def solution(mesh):
    fine = Mesh(mesh.devices.reshape(4, 4, 4, 2), AXES)
    mapped = jax.shard_map(
        body, mesh=fine, in_specs=P(AXES), out_specs=P(AXES), check_vma=False
    )

    def run(*arrays):
        return mapped(jnp.asarray(ring_positions()), *arrays)

    return run
```

```python
import jax
import jax.numpy as jnp
import numpy as np
from jax import lax
from jax.experimental import pallas as pl
from jax.experimental.pallas import tpu as pltpu
from jax.sharding import Mesh, PartitionSpec as P

AXES = ("y", "z", "x", "c")
OFFSETS = (0, 3, 1, 2)
STEPS = (0, 1, 3, 2)
TAIL = 16
BF16 = jnp.bfloat16
BRIEF = pl.CostEstimate(flops=1, bytes_accessed=1, transcendentals=0)
LONG = pl.CostEstimate(flops=10**12, bytes_accessed=1, transcendentals=0)


def ring_positions():
    rows = []
    for y, z, x, c in np.ndindex(4, 4, 4, 2):
        rows.append(
            [(z + o) % 4 for o in OFFSETS]
            + [(x + o) % 4 for o in OFFSETS]
            + [c]
            + [(x + o) % 4 for o in STEPS]
        )
    return np.asarray(rows, np.int32)


def exchange(array, axis):
    return lax.all_to_all(array, axis, split_axis=0, concat_axis=0, tiled=True)


def shift(array, axis, step, size=4):
    return lax.ppermute(array, axis, [(i, (i + step) % size) for i in range(size)])


def both_ways(array, axis):
    return shift(array, axis, 1), shift(array, axis, 3)


def halves_of(from_low, from_high):
    half = from_low.shape[1] // 2
    return from_low[:, :half], from_high[:, half:]


def onward(halves, axis):
    return shift(halves[0], axis, 1), shift(halves[1], axis, 3)


def combine(where, psis, lefts, rights, first, z_first=0, kept=None, cores=(0, 1)):
    codes = [codes for _, codes in psis]
    psis = [psi for psi, _ in psis]
    width = psis[0].shape[-1]
    columns = psis[0].shape[1]
    depth = sum(a.shape[1] for a in lefts[0][0])
    terms = depth // width
    count = len(lefts)
    left_parts = [a for pair in lefts for group in pair for a in group]
    right_parts = [a for group in rights for a in group]
    steps = len(rights)
    last = steps - 1
    size_out = len(cores) * count
    each = [(core, k) for core in cores for k in range(count)]

    def mine(where):
        return where[9] if columns > 1 else 0

    def pick_of(step, core, k, side, where, codes):
        block = where[z_first + step] * 2 + (where[8] ^ core)
        return codes[k][(block * columns + mine(where)) * 2 + side]

    def kernel(where, *refs):
        codes, refs = refs[:count], list(refs[count:])
        psi_refs = [refs.pop(0) for _ in psis]
        left_refs = [[[refs.pop(0) for _ in group] for group in pair] for pair in lefts]
        right_refs = [[refs.pop(0) for _ in group] for group in rights]
        (out_ref, psi_buf, left_buf, right_buf, partial, out_buf, psi_sems, left_sems, sems, out_sems) = refs[
            kept is not None :
        ]
        step = pl.program_id(0)

        def copy_lefts(needed, go):
            for core, k in each:
                at = core - cores[0]
                pick = pick_of(0, core, k, 0, where, codes)
                pick = pick if needed else 1 - pick
                row = 0
                for n, ref in enumerate(left_refs[k][at]):
                    size = ref.shape[1]
                    copy = pltpu.make_async_copy(
                        ref.at[pick],
                        left_buf.at[k, at, pick, pl.ds(row, size)],
                        left_sems.at[k, at, n, 0 if needed else 1],
                    )
                    copy.start() if go else copy.wait()
                    row += size

        def fetch(n_step, go):
            g = where[z_first + n_step]
            for k in range(count):
                copy = pltpu.make_async_copy(
                    psi_refs[k].at[pl.ds(g * 2, 2), mine(where), pl.ds(0, width)],
                    psi_buf.at[n_step, k],
                    psi_sems.at[n_step, k],
                )
                copy.start() if go else copy.wait()
            for n_block, (core, k) in enumerate(each):
                right = pick_of(n_step, core, k, 1, where, codes)
                row = 0
                for n, ref in enumerate(right_refs[n_step]):
                    size = ref.shape[1]
                    copy = pltpu.make_async_copy(
                        ref.at[right],
                        right_buf.at[n_step, n_block, pl.ds(row, size)],
                        sems.at[n_step, n_block, n],
                    )
                    copy.start() if go else copy.wait()
                    row += size

        def leave(n_step):
            g = where[z_first + n_step]
            to = g * size_out if len(cores) > 1 else (g * 2 + (where[8] ^ cores[0])) * count
            return pltpu.make_async_copy(
                out_buf.at[n_step], out_ref.at[pl.ds(to, size_out)], out_sems.at[n_step]
            )

        @pl.when(step == 0)
        def _():
            copy_lefts(True, True)
            fetch(0, True)
            if steps > 1:
                copy_lefts(False, True)
            for n_step in range(1, steps):
                fetch(n_step, True)
            copy_lefts(True, False)

        if steps > 1:

            @pl.when(step == 1)
            def _():
                copy_lefts(False, False)

        for n_step in range(steps):

            @pl.when(step == n_step)
            def _(n_step=n_step):
                fetch(n_step, False)

        for n_block, (core, k) in enumerate(each):
            left = pick_of(step, core, k, 0, where, codes)
            block = psi_buf[step, k, where[8] ^ core]
            for t in range(terms):
                product = jnp.dot(
                    left_buf[k, core - cores[0], left, t * width : (t + 1) * width],
                    block,
                    preferred_element_type=jnp.float32,
                )
                partial[n_block, :, t * width : (t + 1) * width] = product.astype(BF16)
        for n_block, (core, k) in enumerate(each):
            total = jnp.dot(
                partial[n_block], right_buf[step, n_block], preferred_element_type=jnp.float32
            )
            row = (where[8] ^ core) * count if len(cores) > 1 else 0
            out_buf[step, row + k] = total.astype(BF16)
        for n_step in range(steps):

            @pl.when(step == n_step)
            def _(n_step=n_step):
                leave(n_step).start()

        @pl.when(step == last)
        def _():
            for n_step in range(steps):
                leave(n_step).wait()

    in_place = pl.BlockSpec(memory_space=pl.ANY)
    parts = max(len(group) for group in rights)
    extra = [] if kept is None else [kept]
    operands = [*psis, *left_parts, *right_parts, *extra]
    return pl.pallas_call(
        kernel,
        out_shape=jax.ShapeDtypeStruct((8 * count, width, width), BF16),
        grid_spec=pltpu.PrefetchScalarGridSpec(
            num_scalar_prefetch=1 + count,
            grid=(steps,),
            in_specs=[in_place] * len(operands),
            out_specs=in_place,
            scratch_shapes=[
                pltpu.VMEM((steps, count, 2, width, width), BF16),
                pltpu.VMEM((count, len(cores), 2, depth, width), BF16),
                pltpu.VMEM((steps, len(each), depth, width), BF16),
                pltpu.VMEM((len(each), width, depth), BF16),
                pltpu.VMEM((steps, size_out, width, width), BF16),
                pltpu.SemaphoreType.DMA((steps, count)),
                pltpu.SemaphoreType.DMA((count, len(cores), max(len(pair[0]) for pair in lefts), 2)),
                pltpu.SemaphoreType.DMA((steps, len(each), parts)),
                pltpu.SemaphoreType.DMA((steps,)),
            ],
        ),
        input_output_aliases={count + len(operands): 0} if extra else {},
        compiler_params=pltpu.CompilerParams(
            dimension_semantics=("arbitrary",), vmem_limit_bytes=(26 if count == 1 else 46) * 2**20
        ),
        cost_estimate=BRIEF if first == 3 or z_first else LONG,
        name=f"combine_{first}_{z_first}_{cores[0]}",
    )(where, *codes, *operands)


def assemble(where, pieces):
    width = pieces[0][1].shape[-1]
    counts = [piece.shape[0] // 8 for _, piece in pieces]

    def kernel(where, *refs):
        *piece_refs, out_ref = refs
        for (first, _), count, ref in zip(pieces, counts, piece_refs):
            for k in range(count):
                out_ref[0, where[4 + first + k]] = ref[0, :, k]

    at_z = lambda z_j, where: (z_j, 0, 0, 0, 0)
    return pl.pallas_call(
        kernel,
        out_shape=jax.ShapeDtypeStruct((4, 4, 2, width, width), BF16),
        grid_spec=pltpu.PrefetchScalarGridSpec(
            num_scalar_prefetch=1,
            grid=(4,),
            in_specs=[pl.BlockSpec((1, 2, count, width, width), at_z) for count in counts],
            out_specs=pl.BlockSpec((1, 4, 2, width, width), at_z),
        ),
        compiler_params=pltpu.CompilerParams(vmem_limit_bytes=12 * 2**20),
        cost_estimate=BRIEF,
        name="assemble",
    )(where, *[p.reshape(4, 2, n, width, width) for (_, p), n in zip(pieces, counts)])


def pack(wavefunction, pair_left, pair_right):
    width = wavefunction.shape[-1]
    blocks = wavefunction.reshape(4, 4, 2, width, width)

    def kernel(left, right, in_ref, out_ref, buf, in_sems, out_sems):
        copies = []
        for n in range(8):
            copies.append(
                pltpu.make_async_copy(
                    in_ref.at[n // 2, :, n % 2], buf.at[n, :, pl.ds(0, width)], in_sems.at[n]
                )
            )
            copies[n].start()
        lane = lax.broadcasted_iota(jnp.int32, (TAIL, width), 1)
        for n in range(8):
            for x_r in range(4):
                slot = (n // 2 * 4 + x_r) * 2 + n % 2
                picks = jnp.where(lane == 0, left[slot], jnp.where(lane == 1, right[slot], 0))
                buf[n, x_r, width:] = picks.astype(jnp.float32).astype(BF16)
        for n in range(8):
            copies[n].wait()
            copies[n] = pltpu.make_async_copy(buf.at[n], out_ref.at[n], out_sems.at[n])
            copies[n].start()
        for copy in copies:
            copy.wait()

    shape = (8, 4, width + TAIL, width)
    return pl.pallas_call(
        kernel,
        out_shape=jax.ShapeDtypeStruct(shape, BF16),
        grid_spec=pltpu.PrefetchScalarGridSpec(
            num_scalar_prefetch=2,
            grid=(1,),
            in_specs=[pl.BlockSpec(memory_space=pl.ANY)],
            out_specs=pl.BlockSpec(memory_space=pl.ANY),
            scratch_shapes=[
                pltpu.VMEM(shape, BF16),
                pltpu.SemaphoreType.DMA((8,)),
                pltpu.SemaphoreType.DMA((8,)),
            ],
        ),
        compiler_params=pltpu.CompilerParams(vmem_limit_bytes=12 * 2**20),
        cost_estimate=BRIEF,
        name="pack",
    )(pair_left, pair_right, blocks)


def column(psi, position):
    zero = jnp.uint32(0)
    start = (zero, position.astype(jnp.uint32), zero, zero)
    return lax.dynamic_slice(psi, start, (8, 1) + psi.shape[2:])


def split(piece):
    return piece, piece[:, :, -TAIL, :2].astype(jnp.int32).reshape(-1)


def together(*arrays):
    return lax.optimization_barrier(arrays)


def body(where, wavefunction, pair_left, pair_right, left_env, left_dims, right_env, right_dims):
    width = wavefunction.shape[-1]
    sectors, terms = left_env.shape[:2]
    where = where.reshape(-1)

    index = lax.broadcasted_iota(jnp.int32, right_env.shape, 2)
    right_own = jnp.where(index < right_dims[:, None, None, None], right_env, jnp.zeros_like(right_env))
    index = lax.broadcasted_iota(jnp.int32, left_env.shape, 3)
    left_own = jnp.where(index < left_dims[:, None, None, None], left_env, jnp.zeros_like(left_env))
    left_own = left_own.reshape(sectors, terms * width, width)
    right_own = right_own.reshape(sectors, terms * width, width)

    psi = exchange(pack(wavefunction, pair_left, pair_right), ("y", "c"))
    right_low, right_high = both_ways(right_own, "z")
    left_low, left_high = both_ways(left_own, "x")
    left_other = shift(left_own, "c", 1, 2)
    psi, right_low, right_high, left_low, left_high, left_other, *to_far = together(
        psi, right_low, right_high, left_low, left_high, left_other, *halves_of(right_low, right_high)
    )

    for_low, for_high = column(psi, where[10]), column(psi, where[11])
    for_low, for_high, psi, *to_far = together(for_low, for_high, psi, *to_far)
    psi_low, psi_high = shift(for_low, "x", 1), shift(for_high, "x", 3)
    far = onward(to_far, "z")
    psi_own = split(psi)
    rights = [(right_own,), (right_low,), (right_high,)]
    lefts_own = [((left_own,), (left_other,))]
    own = combine(where, [psi_own], lefts_own, rights, 0)
    own, psi, left_low, left_high = together(own, psi, left_low, left_high)
    halves = halves_of(left_low, left_high)
    rights.append(tuple(far))
    own = combine(where, [psi_own], lefts_own, rights[3:], 0, 3, own)
    psi_rest, psi_low, psi_high, own, left_low, left_high, *halves = together(
        column(psi, where[12]), psi_low, psi_high, own, left_low, left_high, *halves
    )

    left_far = onward(halves, "x")
    psi_far = shift(psi_rest, "x", 2)
    own = exchange(own, "z")
    others = [shift(a, "c", 1, 2) for a in (left_low, left_high)]
    psi_low, psi_high, *others = together(psi_low, psi_high, *others)
    lefts_near = [((left_low,), (others[0],)), ((left_high,), (others[1],))]
    near = combine(where, [split(psi_low), split(psi_high)], lefts_near, rights, 1)
    psi_far, *left_far = together(psi_far, *left_far, near)[:-1]
    near = exchange(near, "z")
    other_far = [shift(a, "c", 1, 2) for a in left_far]
    psi_far = split(psi_far)
    rest = combine(where, [psi_far], [(tuple(left_far), tuple(other_far))], rights, 3)
    rest = exchange(rest, "z")
    applied = assemble(where, [(0, own), (1, near)])
    zero = jnp.uint32(0)
    applied = lax.dynamic_update_slice(
        applied,
        rest.reshape(4, 1, 2, width, width),
        (zero, where[7].astype(jnp.uint32), zero, zero, zero),
    )
    return applied.reshape(wavefunction.shape)


def solution(mesh):
    fine = Mesh(mesh.devices.reshape(4, 4, 4, 2), AXES)
    mapped = jax.shard_map(
        body, mesh=fine, in_specs=P(AXES), out_specs=P(AXES), check_vma=False
    )

    def run(*arrays):
        return mapped(jnp.asarray(ring_positions()), *arrays)

    return run
```
